256 devices in a mesh: dp: 4 (over y_lo, core), mp: 64 (over y_hi, z, x).
Axes of the slice: x: 4, y: 4 (y_hi: 2, y_lo: 2; y = y_hi * 2 + y_lo), z: 8, core: 2. Of those that a mesh axis runs over, the one named last changes fastest.
Arguments:
- table: bfloat16 [131072, 1024], P('mp'), may hold values from -200 to 200
- triples: int32 [32, 3], P('dp'), may hold values from 0 to 131071
- words: int32 [32, 61], P('dp'), may hold values from 0 to 131071
- labels: int32 [32], P('dp'), may hold values 0 or 1
- in_gain: float32 [1024], replicated, may hold values from 0.5 to 1.5
- up_weight: bfloat16 [1024, 4096], P(None, 'mp'), may hold values from -0.1875 to 0.1875
- down_weight: bfloat16 [4096, 1024], P('mp'), may hold values from -0.09375 to 0.09375
- out_gain: float32 [1024], P('mp'), may hold values from 0.5 to 1.5
- class_weight: float32 [1024], P('mp'), may hold values from -6 to 6
Outputs:
- encoded: bfloat16 [2048, 1024], P('dp', 'mp')
- scores: float32 [32], P('dp')
- class_grad: float32 [1024], P('mp')
The draws below stay inside these ranges and needn't reach their ends.
All inputs are finite; a program needn't handle non-finite values. No bound on the sum of `labels` on one device may be relied on, other than what follows from the above.
Results may differ from the reference program's by a relative error of at most 0.0075.
Values may be sent and summed in bfloat16 or wider, within the bound.
No kernel may reach another device: no remote copies, remote signals or barrier semaphores. Data moves between devices by JAX's collectives and lax.ppermute only.
A program may use at most 64 MiB of HBM per device.

```python
import jax
import jax.numpy as jnp
from jax import lax

D = 1024
FF = 4096
SEQ = 64
WORDS = 61
ENTITIES = 131072
TRIPLES = 32


def draw_table(key, part):
    first = jax.random.fold_in(key, 0)
    base = jnp.clip(jax.random.normal(first, (ENTITIES, D), jnp.float32), -6.0, 6.0)
    column_scale = jnp.exp(jnp.log(3.0) * jnp.arange(D, dtype=jnp.float32) / D)
    return (base * column_scale[None, :]).astype(jnp.bfloat16)


def plant(entries, own_key, low, top_value):
    longest = entries.shape.index(max(entries.shape))
    spots = []
    for shift in (0, 1):
        where = [jax.random.randint(jax.random.fold_in(own_key, axis), (), 0, length) for axis, length in enumerate(entries.shape)]
        where[longest] = (where[longest] + shift) % entries.shape[longest]
        spots.append(tuple(where))
    return entries.at[spots[0]].set(low).at[spots[1]].set(top_value)


def levels(key, extent, cuts, least, top_value):
    factor_of = 1.0
    for dim, blocks in cuts:
        heights = jax.random.uniform(jax.random.fold_in(jax.random.fold_in(key, 6), dim), (blocks,), jnp.float32, least / len(cuts), top_value / len(cuts))
        factor_of = factor_of * jnp.repeat(jnp.exp(heights), extent[dim] // blocks).reshape((-1,) + (1,) * (len(extent) - 1 - dim))
    return factor_of


def gaussian(key, dims, scale, limit, shards=(), held_as=jnp.bfloat16):
    level = levels(key, dims, shards, -0.22, 0.18) if shards else 1.0
    drawn = jax.random.normal(key, dims, jnp.float32) * scale * level
    return jnp.minimum(jnp.maximum(drawn, -limit), limit).astype(held_as)


def setup_inputs(seed: int = 0) -> dict:
    seeds = jax.random.split(jax.random.key(seed), 10)
    table = draw_table(jax.random.fold_in(seeds[9], 71), 0)
    triples = plant(jax.random.randint(seeds[1], (TRIPLES, 3), 0, ENTITIES), jax.random.fold_in(seeds[1], 1), 0, ENTITIES - 1).astype(jnp.int32)
    words = plant(jax.random.randint(seeds[2], (TRIPLES, WORDS), 0, ENTITIES), jax.random.fold_in(seeds[2], 1), 0, ENTITIES - 1).astype(jnp.int32)
    labels = plant((jax.random.randint(seeds[3], (TRIPLES,), 0, 2) < 1).astype(jnp.int32), jax.random.fold_in(seeds[3], 1), 0, 1)
    in_gain = jnp.clip(1.0 + 0.1 * jax.random.normal(seeds[4], (D,), jnp.float32), 0.5, 1.5)
    up_weight = gaussian(seeds[5], (D, FF), D ** -0.5, 0.1875, ((1, 64),))
    down_weight = gaussian(seeds[6], (FF, D), FF ** -0.5, 0.09375, ((0, 64),))
    out_gain = jnp.clip(1.0 + 0.1 * jax.random.normal(seeds[7], (D,), jnp.float32), 0.5, 1.5)
    class_weight = gaussian(seeds[8], (D,), 1.0, 6.0, ((0, 64),), jnp.float32)
    return dict(table=table, triples=triples, words=words, labels=labels, in_gain=in_gain, up_weight=up_weight, down_weight=down_weight, out_gain=out_gain, class_weight=class_weight)


def norm_rows(values, gain):
    width = values.shape[1]
    mean = lax.optimization_barrier(jnp.sum(values, axis=1)) / width
    var = lax.optimization_barrier(jnp.sum(values * values, axis=1)) / width - mean * mean
    return (values - mean[:, None]) * lax.rsqrt(var + 1e-05)[:, None] * gain

def reference(table, triples, words, labels, in_gain, up_weight, down_weight, out_gain, class_weight):
    ids = jnp.concatenate([triples, words], axis=1).reshape(-1).astype(jnp.int32)
    embed = table[ids].astype(jnp.float32)
    normed = norm_rows(embed, in_gain).astype(jnp.bfloat16)
    hidden = jnp.dot(normed, up_weight, preferred_element_type=jnp.float32)
    active = jax.nn.gelu(hidden, approximate=False).astype(jnp.bfloat16)
    mixed = jnp.dot(active, down_weight, preferred_element_type=jnp.float32)
    resid = normed.astype(jnp.float32) + mixed
    encoded = norm_rows(resid, out_gain).astype(jnp.bfloat16)
    pooled = lax.optimization_barrier(jnp.mean(encoded.astype(jnp.float32).reshape(TRIPLES, SEQ, D), axis=1))
    scores = jnp.dot(pooled, class_weight, precision=lax.Precision.HIGHEST)
    diff = jax.nn.sigmoid(scores) - labels.astype(jnp.float32)
    class_grad = jnp.dot(diff, pooled, precision=lax.Precision.HIGHEST)
    return (encoded, scores, class_grad)
```

```python
import jax
import jax.numpy as jnp
from jax import lax
from jax.sharding import Mesh
from jax.sharding import PartitionSpec as P

MP = ("yh", "z", "x")
DP = ("yl", "core")
ACT = ("yl", "core", "yh", "x")


def exchange(blocks, axes):
    return lax.all_to_all(blocks, axes, split_axis=0, concat_axis=0, tiled=True)


def to_everyone(array, axes):
    return exchange(jnp.broadcast_to(array, (lax.axis_size(axes), *array.shape)), axes)


def rounded(x):
    return lax.reduce_precision(x, exponent_bits=8, mantissa_bits=7)


def thirds(x):
    high = rounded(x)
    middle = rounded(x - high)
    return high, middle, rounded(x - high - middle)


def standardize(values):
    width = values.shape[1]
    mean = jnp.sum(values, axis=1, keepdims=True) / width
    var = jnp.sum(values * values, axis=1, keepdims=True) / width - mean * mean
    return (values - mean) * lax.rsqrt(var + 1e-05)


def on_device(
    table, triples, words, labels, in_gain, up_weight, down_weight, out_gain, class_weight
):
    bf16, f32 = jnp.bfloat16, jnp.float32
    peers = lax.axis_size(MP)
    place = lax.axis_index(MP)
    ids = jnp.concatenate([triples, words], axis=1).reshape(-1)
    seq_len = triples.shape[1] + words.shape[1]
    tok_rows = ids.shape[0]
    width = table.shape[1]
    own_toks = tok_rows // peers
    share = width // peers

    parts = lax.axis_size(DP)
    part = lax.axis_index(DP)
    units = up_weight.shape[1] // parts
    up_part = lax.dynamic_slice_in_dim(up_weight.T, part * units, units, 0)
    down_part = lax.dynamic_slice_in_dim(down_weight, part * units, units, 0)
    weights = to_everyone(jnp.concatenate([up_part, down_part], axis=0), "z")
    up_rows = weights[:, :units].reshape(-1, width)
    down_rows = weights[:, units:].reshape(-1, width)

    entries = table.shape[0]
    local = ids - place * entries
    inside = (local >= 0) & (local < entries)
    picked = jnp.take(table, jnp.clip(local, 0, entries - 1), axis=0)
    picked = jnp.where(inside[:, None], picked, jnp.zeros((), bf16))
    lanes = 128
    per_row = lanes // share
    score_weight = jnp.tile(out_gain * class_weight, per_row)
    here = jnp.arange(lanes) // share == place % per_row
    score_weight = jnp.where(here, score_weight, 0.0)
    extra = jnp.zeros((own_toks, lanes), f32)
    for row, third in enumerate(thirds(score_weight)):
        extra = extra.at[row].set(third)
    extra = jnp.broadcast_to(extra.astype(bf16), (peers, own_toks, lanes))
    sent = jnp.concatenate([picked.reshape(peers, own_toks, width), extra], axis=2)
    got = exchange(sent, MP)
    embed = jnp.sum(got[:, :, :width].astype(f32), axis=0)
    score_weight = got[:, :, width:].astype(f32).reshape(-1, per_row, own_toks, lanes)
    score_weight = jnp.sum(score_weight, axis=(1, 2)).reshape(1, width)

    normed = (standardize(embed) * in_gain).astype(bf16)
    everyone = to_everyone(normed, ACT)
    hidden = lax.dot_general(
        everyone.reshape(-1, width), up_rows, (((1,), (1,)), ((), ())), preferred_element_type=f32
    )
    active = jax.nn.gelu(hidden, approximate=False).astype(bf16)
    terms = jnp.dot(active, down_rows, preferred_element_type=f32).astype(bf16)
    terms = exchange(terms.reshape(everyone.shape), ACT)
    resid = normed.astype(f32) + jnp.sum(terms.astype(f32), axis=0)
    level = standardize(resid)
    score = jnp.sum(level * score_weight) / seq_len

    blocks = level.reshape(own_toks, peers, share).transpose(1, 0, 2).reshape(peers, 1, -1)
    sent = jnp.concatenate([blocks, jnp.full_like(blocks, score)], axis=1)
    got = exchange(sent, MP)
    encoded = (got[:, 0].reshape(tok_rows, share) * out_gain).astype(bf16)
    scores = jnp.sum(got[:, 1, 0].reshape(tok_rows // seq_len, -1), axis=1)
    pooled = jnp.mean(
        encoded.astype(f32).reshape(tok_rows // seq_len, seq_len, share), axis=1
    )
    diff = jax.nn.sigmoid(scores) - labels.astype(f32)
    grad = jnp.sum(diff[:, None] * pooled, axis=0)
    grad = grad + lax.ppermute(grad, "core", [(0, 1), (1, 0)])
    grad = grad + lax.ppermute(grad, "yl", [(0, 1), (1, 0)])
    return encoded, scores, grad


def solution(mesh):
    parts = Mesh(mesh.devices.reshape(2, 2, 2, 8, 4), ("yl", "core", "yh", "z", "x"))
    return jax.shard_map(
        on_device,
        mesh=parts,
        in_specs=(
            P(MP, None),
            P(DP, None),
            P(DP, None),
            P(DP),
            P(),
            P(None, MP),
            P(MP, None),
            P(MP),
            P(MP),
        ),
        out_specs=(P(DP, MP), P(DP), P(MP)),
        check_vma=False,
    )
```

```python
import jax
import jax.numpy as jnp
from jax import lax
from jax.sharding import Mesh
from jax.sharding import PartitionSpec as P

MP = ("yh", "z", "x")
DP = ("yl", "core")
ACT = ("yl", "core", "yh", "x")
LANES = 128


def exchange(blocks, axes):
    return lax.all_to_all(blocks, axes, split_axis=0, concat_axis=0, tiled=True)


def to_everyone(array, axes):
    return exchange(jnp.broadcast_to(array, (lax.axis_size(axes), *array.shape)), axes)


def shifted(array, axis):
    peers = lax.axis_size(axis)
    return [array] + [
        lax.ppermute(array, axis, [(i, (i + step) % peers) for i in range(peers)])
        for step in range(1, peers)
    ]


def swapped(array, axis):
    return lax.ppermute(array, axis, [(0, 1), (1, 0)])


def rounded(x):
    return lax.reduce_precision(x, exponent_bits=8, mantissa_bits=7)


def thirds(x):
    high = rounded(x)
    middle = rounded(x - high)
    return high, middle, rounded(x - high - middle)


def standardize(values):
    width = values.shape[1]
    mean = jnp.sum(values, axis=1, keepdims=True) / width
    var = jnp.sum(values * values, axis=1, keepdims=True) / width - mean * mean
    return (values - mean) * lax.rsqrt(var + 1e-05)


def on_device(
    table, triples, words, labels, in_gain, up_weight, down_weight, out_gain, class_weight
):
    bf16, f32 = jnp.bfloat16, jnp.float32
    peers = lax.axis_size(MP)
    place = lax.axis_index(MP)
    ids = jnp.concatenate([triples, words], axis=1).reshape(1, -1)
    seq_len = triples.shape[1] + words.shape[1]
    toks = ids.shape[1]
    entries, width = table.shape
    slots = toks // peers
    share = width // peers

    owner = ids // entries
    key = owner * toks + jnp.arange(toks)[None]
    spot = jnp.sum(key.reshape(-1, 1) < key, axis=0, keepdims=True)
    first = jnp.sum(owner.reshape(-1, 1) < owner, axis=0, keepdims=True)
    trip = (spot - first) // peers
    trips = jnp.max(trip) + 1
    trips = jnp.maximum(trips, swapped(trips, "core"))
    trips = jnp.maximum(trips, swapped(trips, "yl"))
    mine = owner == place
    to_peer = (spot % peers == jnp.arange(peers)[:, None]) & mine
    kept = spot == jnp.arange(slots)[:, None] * peers + place
    sender = jnp.sum(jnp.where(kept, owner, 0), axis=1, keepdims=True)
    sent_in = jnp.sum(jnp.where(kept, trip, 0), axis=1, keepdims=True)
    from_peer = sender == jnp.arange(peers)[None]

    def rows_of(now):
        chosen = to_peer & (trip == now)
        local = jnp.sum(jnp.where(chosen, ids - place * entries, 0), axis=1)
        return jnp.take(table, local, axis=0, mode="clip").reshape(peers, 1, width)

    def taken(now, rows):
        picks = (from_peer & (sent_in == now)).astype(bf16)
        return jnp.dot(picks, rows, preferred_element_type=f32)

    score_weight = jnp.concatenate(thirds(out_gain * class_weight)).astype(bf16)
    score_weight = jnp.pad(score_weight, (0, width - score_weight.size))
    extra = jnp.broadcast_to(score_weight, (peers, 1, width))
    got = exchange(jnp.concatenate([rows_of(0), extra], axis=1), MP)
    embed = taken(0, got[:, 0])
    score_weight = got[:, 1, : 3 * share].astype(f32).reshape(peers, 3, share)
    score_weight = jnp.sum(score_weight, axis=1).reshape(1, width)

    parts = lax.axis_size(DP)
    part = lax.axis_index(DP)
    units = up_weight.shape[1] // parts
    up_part = lax.dynamic_slice_in_dim(up_weight.T, part * units, units, 0)
    down_part = lax.dynamic_slice_in_dim(down_weight, part * units, units, 0)
    weights = shifted(jnp.concatenate([up_part, down_part], axis=0), "z")
    up_rows = jnp.concatenate([w[:units] for w in weights], axis=0)
    down_rows = jnp.concatenate([w[units:] for w in weights], axis=0)

    def another(state):
        now, embed = state
        return now + 1, embed + taken(now, exchange(rows_of(now), MP)[:, 0])

    _, embed = lax.while_loop(lambda state: state[0] < trips, another, (jnp.int32(1), embed))

    normed = (standardize(embed) * in_gain).astype(bf16)
    everyone = to_everyone(normed, ACT)
    hidden = lax.dot_general(
        everyone.reshape(-1, width), up_rows, (((1,), (1,)), ((), ())), preferred_element_type=f32
    )
    active = jax.nn.gelu(hidden, approximate=False).astype(bf16)
    terms = jnp.dot(active, down_rows, preferred_element_type=f32).astype(bf16)
    terms = exchange(terms.reshape(everyone.shape), ACT)
    resid = normed.astype(f32) + jnp.sum(terms.astype(f32), axis=0)
    level = standardize(resid)
    score = jnp.sum(level * score_weight, axis=1)

    blocks = level.reshape(slots, peers, share).transpose(1, 0, 2).reshape(peers, 1, -1)
    score = jnp.broadcast_to(jnp.pad(score, (0, LANES - slots)), (peers, 1, LANES))
    got = exchange(jnp.concatenate([blocks, score], axis=2), MP)
    level = got[:, 0, : slots * share].reshape(peers, slots, share)
    by_spot = (level * out_gain).astype(bf16).transpose(1, 0, 2).reshape(toks, share)
    score = got[:, 0, slots * share :][:, :slots].T.reshape(1, toks)
    where = spot == jnp.arange(toks)[:, None]
    encoded = lax.dot_general(
        by_spot, where.astype(bf16), (((0,), (0,)), ((), ())), preferred_element_type=f32
    )
    triple = jnp.arange(toks // seq_len)[:, None]
    of_triple = jnp.sum(jnp.where(where, jnp.arange(toks)[None] // seq_len, 0), axis=1)
    scores = jnp.sum(jnp.where(of_triple[None] == triple, score, 0.0), axis=1) / seq_len
    diff = jax.nn.sigmoid(scores) - labels.astype(f32)
    pooled = jnp.mean(encoded.reshape(share, toks // seq_len, seq_len), axis=2)
    grad = jnp.sum(diff[None] * pooled, axis=1)
    grad = grad + swapped(grad, "core")
    grad = grad + swapped(grad, "yl")
    return encoded.T.astype(bf16), scores, grad


def solution(mesh):
    parts = Mesh(mesh.devices.reshape(2, 2, 2, 8, 4), ("yl", "core", "yh", "z", "x"))
    return jax.shard_map(
        on_device,
        mesh=parts,
        in_specs=(
            P(MP, None),
            P(DP, None),
            P(DP, None),
            P(DP),
            P(),
            P(None, MP),
            P(MP, None),
            P(MP),
            P(MP),
        ),
        out_specs=(P(DP, MP), P(DP), P(MP)),
        check_vma=False,
    )
```

```python
import jax
import jax.numpy as jnp
from jax import lax
from jax.sharding import Mesh
from jax.sharding import PartitionSpec as P

MP = ("yh", "z", "x")
DP = ("yl", "core")
ACT = ("core", "yh", "x")
LANES = 128


def exchange(blocks, axes):
    return lax.all_to_all(blocks, axes, split_axis=0, concat_axis=0, tiled=True)


def to_everyone(array, axes):
    return exchange(jnp.broadcast_to(array, (lax.axis_size(axes), *array.shape)), axes)


def swapped(array, axis):
    return lax.ppermute(array, axis, [(0, 1), (1, 0)])


def rounded(x):
    return lax.reduce_precision(x, exponent_bits=8, mantissa_bits=7)


def thirds(x):
    high = rounded(x)
    middle = rounded(x - high)
    return high, middle, rounded(x - high - middle)


def standardize(values):
    width = values.shape[1]
    mean = jnp.sum(values, axis=1, keepdims=True) / width
    var = jnp.sum(values * values, axis=1, keepdims=True) / width - mean * mean
    return (values - mean) * lax.rsqrt(var + 1e-05)


def on_device(
    table, triples, words, labels, in_gain, up_weight, down_weight, out_gain, class_weight
):
    bf16, f32 = jnp.bfloat16, jnp.float32
    peers = lax.axis_size(MP)
    place = lax.axis_index(MP)
    ids = jnp.concatenate([triples, words], axis=1).reshape(1, -1)
    seq_len = triples.shape[1] + words.shape[1]
    toks = ids.shape[1]
    entries, width = table.shape
    slots = toks // peers
    share = width // peers

    owner = ids // entries
    key = owner * toks + jnp.arange(toks)[None]
    spot = jnp.sum(key.reshape(-1, 1) < key, axis=0, keepdims=True)
    first = jnp.sum(owner.reshape(-1, 1) < owner, axis=0, keepdims=True)
    trip = (spot - first) // peers
    trips = jnp.max(trip) + 1
    trips = jnp.maximum(trips, swapped(trips, "core"))
    trips = jnp.maximum(trips, swapped(trips, "yl"))
    mine = owner == place
    to_peer = (spot % peers == jnp.arange(peers)[:, None]) & mine
    kept = spot == jnp.arange(slots)[:, None] * peers + place
    sender = jnp.sum(jnp.where(kept, owner, 0), axis=1, keepdims=True)
    sent_in = jnp.sum(jnp.where(kept, trip, 0), axis=1, keepdims=True)
    from_peer = sender == jnp.arange(peers)[None]

    def rows_of(now):
        chosen = to_peer & (trip == now)
        local = jnp.sum(jnp.where(chosen, ids - place * entries, 0), axis=1)
        return jnp.take(table, local, axis=0, mode="clip").reshape(peers, 1, width)

    def taken(now, rows):
        picks = (from_peer & (sent_in == now)).astype(bf16)
        return jnp.dot(picks, rows, preferred_element_type=f32)

    score_weight = jnp.concatenate(thirds(out_gain * class_weight)).astype(bf16)
    score_weight = jnp.pad(score_weight, (0, width - score_weight.size))
    extra = jnp.broadcast_to(score_weight, (peers, 1, width))
    got = exchange(jnp.concatenate([rows_of(0), extra], axis=1), MP)
    embed = taken(0, got[:, 0])
    score_weight = got[:, 1, : 3 * share].astype(f32).reshape(peers, 3, share)
    score_weight = jnp.sum(score_weight, axis=1).reshape(1, width)

    halves = lax.axis_size("core")
    half = lax.axis_index("core")
    units = up_weight.shape[1] // halves
    up_part = lax.dynamic_slice_in_dim(up_weight.T, half * units, units, 0)
    down_part = lax.dynamic_slice_in_dim(down_weight, half * units, units, 0)
    weights = lax.all_gather(jnp.concatenate([up_part, down_part], axis=0), "z", axis=0)
    up_rows = weights[:, :units].reshape(-1, width)
    down_rows = weights[:, units:].reshape(-1, width)

    def another(state):
        now, embed = state
        return now + 1, embed + taken(now, exchange(rows_of(now), MP)[:, 0])

    _, embed = lax.while_loop(lambda state: state[0] < trips, another, (jnp.int32(1), embed))

    normed = (standardize(embed) * in_gain).astype(bf16)
    everyone = to_everyone(normed, ACT)
    hidden = lax.dot_general(
        everyone.reshape(-1, width), up_rows, (((1,), (1,)), ((), ())), preferred_element_type=f32
    )
    active = jax.nn.gelu(hidden, approximate=False).astype(bf16)
    terms = jnp.dot(active, down_rows, preferred_element_type=f32).astype(bf16)
    terms = exchange(terms.reshape(everyone.shape), ACT)
    resid = normed.astype(f32) + jnp.sum(terms.astype(f32), axis=0)
    level = standardize(resid)
    score = jnp.sum(level * score_weight, axis=1)

    blocks = level.reshape(slots, peers, share).transpose(1, 0, 2).reshape(peers, 1, -1)
    score = jnp.broadcast_to(jnp.pad(score, (0, LANES - slots)), (peers, 1, LANES))
    got = exchange(jnp.concatenate([blocks, score], axis=2), MP)
    level = got[:, 0, : slots * share].reshape(peers, slots, share)
    by_spot = (level * out_gain).astype(bf16).transpose(1, 0, 2).reshape(toks, share)
    score = got[:, 0, slots * share :][:, :slots].T.reshape(1, toks)
    where = spot == jnp.arange(toks)[:, None]
    encoded = lax.dot_general(
        by_spot, where.astype(bf16), (((0,), (0,)), ((), ())), preferred_element_type=f32
    )
    triple = jnp.arange(toks // seq_len)[:, None]
    of_triple = jnp.sum(jnp.where(where, jnp.arange(toks)[None] // seq_len, 0), axis=1)
    scores = jnp.sum(jnp.where(of_triple[None] == triple, score, 0.0), axis=1) / seq_len
    diff = jax.nn.sigmoid(scores) - labels.astype(f32)
    pooled = jnp.mean(encoded.reshape(share, toks // seq_len, seq_len), axis=2)
    grad = jnp.sum(diff[None] * pooled, axis=1)
    grad = grad + swapped(grad, "core")
    grad = grad + swapped(grad, "yl")
    return encoded.T.astype(bf16), scores, grad


def solution(mesh):
    parts = Mesh(mesh.devices.reshape(2, 2, 2, 8, 4), ("yl", "core", "yh", "z", "x"))
    return jax.shard_map(
        on_device,
        mesh=parts,
        in_specs=(
            P(MP, None),
            P(DP, None),
            P(DP, None),
            P(DP),
            P(),
            P(None, MP),
            P(MP, None),
            P(MP),
            P(MP),
        ),
        out_specs=(P(DP, MP), P(DP), P(MP)),
        check_vma=False,
    )
```

```python
import jax
import jax.numpy as jnp
from jax import lax
from jax.sharding import Mesh
from jax.sharding import PartitionSpec as P

MP = ("yh", "zh", "zl", "x")
DP = ("yl", "core")
ACT = ("yh", "zl", "x")
LANES = 128


def exchange(blocks, axes):
    return lax.all_to_all(blocks, axes, split_axis=0, concat_axis=0, tiled=True)


def to_everyone(array, axes):
    return exchange(jnp.broadcast_to(array, (lax.axis_size(axes), *array.shape)), axes)


def from_column(array):
    steps, places = lax.axis_size("zh"), lax.axis_size(DP)
    moves = [
        (d * steps + (i + d) % steps, d * steps + i) for d in range(places) for i in range(steps)
    ]
    return lax.ppermute(array, (*DP, "zh"), moves)


def swapped(array, axis):
    return lax.ppermute(array, axis, [(0, 1), (1, 0)])


def rounded(x):
    return lax.reduce_precision(x, exponent_bits=8, mantissa_bits=7)


def thirds(x):
    high = rounded(x)
    middle = rounded(x - high)
    return high, middle, rounded(x - high - middle)


def standardize(values):
    width = values.shape[1]
    mean = jnp.sum(values, axis=1, keepdims=True) / width
    var = jnp.sum(values * values, axis=1, keepdims=True) / width - mean * mean
    return (values - mean) * lax.rsqrt(var + 1e-05)


def on_device(
    table, triples, words, labels, in_gain, up_weight, down_weight, out_gain, class_weight
):
    bf16, f32 = jnp.bfloat16, jnp.float32
    peers = lax.axis_size(MP)
    place = lax.axis_index(MP)
    ids = jnp.concatenate([triples, words], axis=1).reshape(1, -1)
    seq_len = triples.shape[1] + words.shape[1]
    toks = ids.shape[1]
    entries, width = table.shape
    slots = toks // peers
    share = width // peers

    owner = ids // entries
    key = owner * toks + jnp.arange(toks)[None]
    spot = jnp.sum(key.reshape(-1, 1) < key, axis=0, keepdims=True)
    first = jnp.sum(owner.reshape(-1, 1) < owner, axis=0, keepdims=True)
    trip = (spot - first) // peers
    trips = jnp.max(trip) + 1
    trips = jnp.maximum(trips, swapped(trips, "core"))
    trips = jnp.maximum(trips, swapped(trips, "yl"))
    mine = owner == place
    to_peer = (spot % peers == jnp.arange(peers)[:, None]) & mine
    kept = spot == jnp.arange(slots)[:, None] * peers + place
    sender = jnp.sum(jnp.where(kept, owner, 0), axis=1, keepdims=True)
    sent_in = jnp.sum(jnp.where(kept, trip, 0), axis=1, keepdims=True)
    from_peer = sender == jnp.arange(peers)[None]

    def rows_of(now):
        chosen = to_peer & (trip == now)
        local = jnp.sum(jnp.where(chosen, ids - place * entries, 0), axis=1)
        return jnp.take(table, local, axis=0, mode="clip").reshape(peers, 1, width)

    def taken(now, rows):
        picks = (from_peer & (sent_in == now)).astype(bf16)
        return jnp.dot(picks, rows, preferred_element_type=f32)

    units = up_weight.shape[1]
    weights = from_column(jnp.concatenate([up_weight.T, down_weight], axis=0))

    score_weight = jnp.concatenate(thirds(out_gain * class_weight)).astype(bf16)
    score_weight = jnp.pad(score_weight, (0, width - score_weight.size))
    extra = jnp.broadcast_to(score_weight, (peers, 1, width))
    got = exchange(jnp.concatenate([rows_of(0), extra], axis=1), MP)
    embed = taken(0, got[:, 0])
    score_weight = got[:, 1, : 3 * share].astype(f32).reshape(peers, 3, share)
    score_weight = jnp.sum(score_weight, axis=1).reshape(1, width)

    def another(state):
        now, embed = state
        return now + 1, embed + taken(now, exchange(rows_of(now), MP)[:, 0])

    _, embed = lax.while_loop(lambda state: state[0] < trips, another, (jnp.int32(1), embed))

    weights = jnp.where(embed[0, 0] < jnp.inf, weights, 0)[None]
    weights = jnp.concatenate([weights, swapped(weights, "core")], axis=0)
    weights = jnp.concatenate([weights, swapped(weights, "yl")], axis=0)
    up_rows = weights[:, :units].reshape(-1, width)
    down_rows = weights[:, units:].reshape(-1, width)

    normed = (standardize(embed) * in_gain).astype(bf16)
    everyone = to_everyone(normed, ACT)
    hidden = lax.dot_general(
        everyone.reshape(-1, width), up_rows, (((1,), (1,)), ((), ())), preferred_element_type=f32
    )
    active = jax.nn.gelu(hidden, approximate=False).astype(bf16)
    terms = jnp.dot(active, down_rows, preferred_element_type=f32).astype(bf16)
    terms = exchange(terms.reshape(everyone.shape), ACT)
    resid = normed.astype(f32) + jnp.sum(terms.astype(f32), axis=0)
    level = standardize(resid)
    score = jnp.sum(level * score_weight, axis=1)

    blocks = level.reshape(slots, peers, share).transpose(1, 0, 2).reshape(peers, 1, -1)
    score = jnp.broadcast_to(jnp.pad(score, (0, LANES - slots)), (peers, 1, LANES))
    got = exchange(jnp.concatenate([blocks, score], axis=2), MP)
    level = got[:, 0, : slots * share].reshape(peers, slots, share)
    by_spot = (level * out_gain).astype(bf16).transpose(1, 0, 2).reshape(toks, share)
    score = got[:, 0, slots * share :][:, :slots].T.reshape(1, toks)
    where = spot == jnp.arange(toks)[:, None]
    encoded = lax.dot_general(
        by_spot, where.astype(bf16), (((0,), (0,)), ((), ())), preferred_element_type=f32
    )
    triple = jnp.arange(toks // seq_len)[:, None]
    of_triple = jnp.sum(jnp.where(where, jnp.arange(toks)[None] // seq_len, 0), axis=1)
    scores = jnp.sum(jnp.where(of_triple[None] == triple, score, 0.0), axis=1) / seq_len
    diff = jax.nn.sigmoid(scores) - labels.astype(f32)
    pooled = jnp.mean(encoded.reshape(share, toks // seq_len, seq_len), axis=2)
    grad = jnp.sum(diff[None] * pooled, axis=1)
    grad = grad + swapped(grad, "core")
    grad = grad + swapped(grad, "yl")
    return encoded.T.astype(bf16), scores, grad


def solution(mesh):
    parts = Mesh(mesh.devices.reshape(2, 2, 2, 4, 2, 4), (*DP, *MP))
    return jax.shard_map(
        on_device,
        mesh=parts,
        in_specs=(
            P(MP, None),
            P(DP, None),
            P(DP, None),
            P(DP),
            P(),
            P(None, MP),
            P(MP, None),
            P(MP),
            P(MP),
        ),
        out_specs=(P(DP, MP), P(DP), P(MP)),
        check_vma=False,
    )
```

```python
import jax
import jax.numpy as jnp
from jax import lax
from jax.sharding import Mesh
from jax.sharding import PartitionSpec as P

MP = ("yh", "zh", "zl", "x")
DP = ("yl", "core")
ACT = ("yh", "zl", "x")
LANES = 128


def exchange(blocks, axes):
    return lax.all_to_all(blocks, axes, split_axis=0, concat_axis=0, tiled=True)


def to_everyone(array, axes):
    return exchange(jnp.broadcast_to(array, (lax.axis_size(axes), *array.shape)), axes)


def from_column(array, axis):
    peers = lax.axis_size(axis)
    return [array] + [
        lax.ppermute(array, axis, [((i + step) % peers, i) for i in range(peers)])
        for step in range(1, peers)
    ]


def swapped(array, axis):
    return lax.ppermute(array, axis, [(0, 1), (1, 0)])


def rounded(x):
    return lax.reduce_precision(x, exponent_bits=8, mantissa_bits=7)


def thirds(x):
    high = rounded(x)
    middle = rounded(x - high)
    return high, middle, rounded(x - high - middle)


def standardize(values):
    width = values.shape[1]
    mean = jnp.sum(values, axis=1, keepdims=True) / width
    var = jnp.sum(values * values, axis=1, keepdims=True) / width - mean * mean
    return (values - mean) * lax.rsqrt(var + 1e-05)


def on_device(
    table, triples, words, labels, in_gain, up_weight, down_weight, out_gain, class_weight
):
    bf16, f32 = jnp.bfloat16, jnp.float32
    peers = lax.axis_size(MP)
    place = lax.axis_index(MP)
    ids = jnp.concatenate([triples, words], axis=1).reshape(1, -1)
    seq_len = triples.shape[1] + words.shape[1]
    toks = ids.shape[1]
    entries, width = table.shape
    slots = toks // peers
    share = width // peers

    owner = ids // entries
    key = owner * toks + jnp.arange(toks)[None]
    spot = jnp.sum(key.reshape(-1, 1) < key, axis=0, keepdims=True)
    first = jnp.sum(owner.reshape(-1, 1) < owner, axis=0, keepdims=True)
    trip = (spot - first) // peers
    trips = jnp.max(trip) + 1
    trips = jnp.maximum(trips, swapped(trips, "core"))
    trips = jnp.maximum(trips, swapped(trips, "yl"))
    mine = owner == place
    to_peer = (spot % peers == jnp.arange(peers)[:, None]) & mine
    kept = spot == jnp.arange(slots)[:, None] * peers + place
    sender = jnp.sum(jnp.where(kept, owner, 0), axis=1, keepdims=True)
    sent_in = jnp.sum(jnp.where(kept, trip, 0), axis=1, keepdims=True)
    from_peer = sender == jnp.arange(peers)[None]

    def rows_of(now):
        chosen = to_peer & (trip == now)
        local = jnp.sum(jnp.where(chosen, ids - place * entries, 0), axis=1)
        return jnp.take(table, local, axis=0, mode="clip").reshape(peers, 1, width)

    def taken(now, rows):
        picks = (from_peer & (sent_in == now)).astype(bf16)
        return jnp.dot(picks, rows, preferred_element_type=f32)

    units = up_weight.shape[1]
    weights = from_column(jnp.concatenate([up_weight.T, down_weight], axis=0), "zh")
    up_rows = jnp.concatenate([w[:units] for w in weights], axis=0)
    down_rows = jnp.concatenate([w[units:] for w in weights], axis=0)

    score_weight = jnp.concatenate(thirds(out_gain * class_weight)).astype(bf16)
    score_weight = jnp.pad(score_weight, (0, width - score_weight.size))
    extra = jnp.broadcast_to(score_weight, (peers, 1, width))
    got = exchange(jnp.concatenate([rows_of(0), extra], axis=1), MP)
    embed = taken(0, got[:, 0])
    score_weight = got[:, 1, : 3 * share].astype(f32).reshape(peers, 3, share)
    score_weight = jnp.sum(score_weight, axis=1).reshape(1, width)

    def another(state):
        now, embed = state
        return now + 1, embed + taken(now, exchange(rows_of(now), MP)[:, 0])

    _, embed = lax.while_loop(lambda state: state[0] < trips, another, (jnp.int32(1), embed))

    normed = (standardize(embed) * in_gain).astype(bf16)
    everyone = to_everyone(normed, ACT)
    hidden = lax.dot_general(
        everyone.reshape(-1, width), up_rows, (((1,), (1,)), ((), ())), preferred_element_type=f32
    )
    active = jax.nn.gelu(hidden, approximate=False).astype(bf16)
    terms = jnp.dot(active, down_rows, preferred_element_type=f32).astype(bf16)
    terms = exchange(terms.reshape(everyone.shape), ACT)
    resid = normed.astype(f32) + jnp.sum(terms.astype(f32), axis=0)
    level = standardize(resid)
    score = jnp.sum(level * score_weight, axis=1)

    blocks = level.reshape(slots, peers, share).transpose(1, 0, 2).reshape(peers, 1, -1)
    score = jnp.broadcast_to(jnp.pad(score, (0, LANES - slots)), (peers, 1, LANES))
    got = exchange(jnp.concatenate([blocks, score], axis=2), MP)
    level = got[:, 0, : slots * share].reshape(peers, slots, share)
    by_spot = (level * out_gain).astype(bf16).transpose(1, 0, 2).reshape(toks, share)
    score = got[:, 0, slots * share :][:, :slots].T.reshape(1, toks)
    where = spot == jnp.arange(toks)[:, None]
    encoded = lax.dot_general(
        by_spot, where.astype(bf16), (((0,), (0,)), ((), ())), preferred_element_type=f32
    )
    triple = jnp.arange(toks // seq_len)[:, None]
    of_triple = jnp.sum(jnp.where(where, jnp.arange(toks)[None] // seq_len, 0), axis=1)
    scores = jnp.sum(jnp.where(of_triple[None] == triple, score, 0.0), axis=1) / seq_len
    diff = jax.nn.sigmoid(scores) - labels.astype(f32)
    pooled = jnp.mean(encoded.reshape(share, toks // seq_len, seq_len), axis=2)
    grad = jnp.sum(diff[None] * pooled, axis=1)
    grad = grad + swapped(grad, "core")
    grad = grad + swapped(grad, "yl")
    return encoded.T.astype(bf16), scores, grad


def solution(mesh):
    parts = Mesh(mesh.devices.reshape(2, 2, 2, 4, 2, 4), (*DP, *MP))
    return jax.shard_map(
        on_device,
        mesh=parts,
        in_specs=(
            P(MP, None),
            P(DP, None),
            P(DP, None),
            P(DP),
            P(),
            P(None, MP),
            P(MP, None),
            P(MP),
            P(MP),
        ),
        out_specs=(P(DP, MP), P(DP), P(MP)),
        check_vma=False,
    )
```

```python
import functools

import jax
import jax.numpy as jnp
from jax import lax
from jax.experimental import pallas as pl
from jax.experimental.pallas import tpu as pltpu
from jax.sharding import Mesh
from jax.sharding import PartitionSpec as P

MP = ("yh", "zh", "zl", "x")
DP = ("yl", "core")
ACT = ("yh", "zl", "x")
LANES = 128


def exchange(blocks, axes):
    return lax.all_to_all(blocks, axes, split_axis=0, concat_axis=0, tiled=True)


def to_everyone(array, axes):
    return exchange(jnp.broadcast_to(array, (lax.axis_size(axes), *array.shape)), axes)


def from_column(array, axis):
    peers = lax.axis_size(axis)
    return [array] + [
        lax.ppermute(array, axis, [((i + step) % peers, i) for i in range(peers)])
        for step in range(1, peers)
    ]


def swapped(array, axis):
    return lax.ppermute(array, axis, [(0, 1), (1, 0)])


def gather_kernel(
    peers, place_ref, triples, words, triples_v, words_v, gain, weight, table,
    sent, spot_ref, tiles, ids, lanes, rows, sems,
):
    place = place_ref[0]
    n_triples, seq_len = ids.shape
    lead = triples.shape[1]
    toks = n_triples * seq_len
    entries, width = table.shape
    half = width // 2
    shift = entries.bit_length() - 1
    low = place * entries

    lanes[...] = jnp.zeros_like(lanes)
    share = gain.shape[1]
    lanes[0:1, 0:share] = gain[...] * weight[...]
    exact = lanes[...]
    high = exact.astype(jnp.bfloat16).astype(jnp.float32)
    middle = (exact - high).astype(jnp.bfloat16).astype(jnp.float32)
    least = (exact - high - middle).astype(jnp.bfloat16).astype(jnp.float32)
    parts = high + pltpu.roll(middle, share, 1) + pltpu.roll(least, 2 * share, 1)
    sent[:, :, 0:half] = jnp.zeros((peers, 2, half), sent.dtype)
    sent[:, :, half:] = jnp.broadcast_to(parts[None, 0:2], (peers, 2, LANES)).astype(sent.dtype)

    ids[:, 0:lead] = triples_v[...]
    ids[:, lead:] = words_v[...]
    order = lax.broadcasted_iota(jnp.int32, ids.shape, 0) * seq_len
    order = order + lax.broadcasted_iota(jnp.int32, ids.shape, 1)
    keys = (ids[...] >> shift) * toks + order

    def copy(number, local):
        start = pl.multiple_of((local >> 3) * 8, 8)
        return pltpu.make_async_copy(
            table.at[pl.ds(start, 8), :], tiles.at[number], sems.at[number]
        )

    def scan(i, carry):
        spot, first, held = carry
        for j in range(seq_len):
            token = triples[i, j] if j < lead else words[i, j - lead]
            key = (token >> shift) * toks + (i * seq_len + j)
            spot = spot + (key < keys).astype(jnp.int32)
            local = token - low
            mine = (local >= 0) & (local < entries)

            @pl.when(mine & (held < peers))
            def _(local=local, held=held):
                rows[held] = local
                copy(held, local).start()

            first = first + (local < 0).astype(jnp.int32)
            held = held + mine.astype(jnp.int32)
        return spot, first, held

    zero = jnp.int32(0)
    spot, first, held = lax.fori_loop(
        0, n_triples, scan, (jnp.zeros(ids.shape, jnp.int32), zero, zero)
    )
    spot_ref[...] = spot

    def place_row(number, carry):
        local = rows[number]
        copy(number, local).wait()
        tile = tiles[number].astype(jnp.float32)
        here = lax.broadcasted_iota(jnp.int32, tile.shape, 0) == (local & 7)
        row = jnp.sum(jnp.where(here, tile, 0.0), axis=0, keepdims=True)
        peer = (first + number) & (peers - 1)
        pair = jnp.concatenate([row[:, :half], row[:, half:]], axis=0)
        sent[peer, :, 0:half] = pair.astype(sent.dtype)
        return carry

    lax.fori_loop(0, jnp.minimum(held, peers), place_row, zero)


def gathered(place, triples, words, gain, weight, table, peers):
    n_triples, seq_len = triples.shape[0], triples.shape[1] + words.shape[1]
    width = table.shape[1]
    vmem = pl.BlockSpec(memory_space=pltpu.VMEM)
    smem = pl.BlockSpec(memory_space=pltpu.SMEM)
    return pl.pallas_call(
        functools.partial(gather_kernel, peers),
        out_shape=(
            jax.ShapeDtypeStruct((peers, 2, width // 2 + LANES), table.dtype),
            jax.ShapeDtypeStruct((n_triples, seq_len), jnp.int32),
        ),
        in_specs=[smem] * 3 + [vmem] * 4 + [pl.BlockSpec(memory_space=pl.ANY)],
        out_specs=(vmem, vmem),
        scratch_shapes=[
            pltpu.VMEM((peers, 8, width), table.dtype),
            pltpu.VMEM((n_triples, seq_len), jnp.int32),
            pltpu.VMEM((8, LANES), jnp.float32),
            pltpu.SMEM((peers,), jnp.int32),
            pltpu.SemaphoreType.DMA((peers,)),
        ],
        name="gather_rows",
    )(place, triples, words, triples, words, gain, weight, table)


def standardize(values):
    width = values.shape[1]
    mean = jnp.sum(values, axis=1, keepdims=True) / width
    var = jnp.sum(values * values, axis=1, keepdims=True) / width - mean * mean
    return (values - mean) * lax.rsqrt(var + 1e-05)


def on_device(
    table, triples, words, labels, in_gain, up_weight, down_weight, out_gain, class_weight
):
    bf16, f32 = jnp.bfloat16, jnp.float32
    peers = lax.axis_size(MP)
    place = lax.axis_index(MP)
    ids = jnp.concatenate([triples, words], axis=1).reshape(1, -1)
    seq_len = triples.shape[1] + words.shape[1]
    toks = ids.shape[1]
    entries, width = table.shape
    slots = toks // peers
    share = width // peers

    sent, spot = gathered(
        place.reshape(1),
        triples,
        words,
        out_gain.reshape(1, -1),
        class_weight.reshape(1, -1),
        table,
        peers,
    )
    got = exchange(sent, MP)

    owner = ids // entries
    spot = spot.reshape(1, toks)
    first = jnp.sum(owner.reshape(-1, 1) < owner, axis=0, keepdims=True)
    trip = (spot - first) // peers
    trips = jnp.max(trip) + 1
    trips = jnp.maximum(trips, swapped(trips, "core"))

    units = up_weight.shape[1]
    weights = jnp.concatenate([up_weight.T, down_weight], axis=0)
    weights = from_column(jnp.where(trips <= toks, weights, 0), "zh")
    up_rows = jnp.concatenate([w[:units] for w in weights], axis=0)
    down_rows = jnp.concatenate([w[units:] for w in weights], axis=0)

    trips = jnp.maximum(trips, swapped(trips, "yl"))
    mine = owner == place
    to_peer = (spot % peers == jnp.arange(peers)[:, None]) & mine
    kept = spot == jnp.arange(slots)[:, None] * peers + place
    sender = jnp.sum(jnp.where(kept, owner, 0), axis=1, keepdims=True)
    sent_in = jnp.sum(jnp.where(kept, trip, 0), axis=1, keepdims=True)
    from_peer = sender == jnp.arange(peers)[None]

    def rows_of(now):
        chosen = to_peer & (trip == now)
        local = jnp.sum(jnp.where(chosen, ids - place * entries, 0), axis=1)
        return jnp.take(table, local, axis=0, mode="clip").reshape(peers, 1, width)

    def taken(now, rows):
        picks = (from_peer & (sent_in == now)).astype(bf16)
        return jnp.dot(picks, rows, preferred_element_type=f32)

    half = width // 2
    embed = taken(0, jnp.concatenate([got[:, 0, :half], got[:, 1, :half]], axis=1))
    score_weight = got[:, 0, half : half + 3 * share].astype(f32).reshape(peers, 3, share)
    score_weight = jnp.sum(score_weight, axis=1).reshape(1, width)

    def another(state):
        now, embed = state
        return now + 1, embed + taken(now, exchange(rows_of(now), MP)[:, 0])

    _, embed = lax.while_loop(lambda state: state[0] < trips, another, (jnp.int32(1), embed))

    normed = (standardize(embed) * in_gain).astype(bf16)
    everyone = to_everyone(normed, ACT)
    hidden = lax.dot_general(
        everyone.reshape(-1, width), up_rows, (((1,), (1,)), ((), ())), preferred_element_type=f32
    )
    active = jax.nn.gelu(hidden, approximate=False).astype(bf16)
    terms = jnp.dot(active, down_rows, preferred_element_type=f32).astype(bf16)
    terms = exchange(terms.reshape(everyone.shape), ACT)
    resid = normed.astype(f32) + jnp.sum(terms.astype(f32), axis=0)
    level = standardize(resid)
    score = jnp.sum(level * score_weight, axis=1)

    blocks = level.reshape(slots, peers, share).transpose(1, 0, 2).reshape(peers, 1, -1)
    score = jnp.broadcast_to(jnp.pad(score, (0, LANES - slots)), (peers, 1, LANES))
    got = exchange(jnp.concatenate([blocks, score], axis=2), MP)
    level = got[:, 0, : slots * share].reshape(peers, slots, share)
    by_spot = (level * out_gain).astype(bf16).transpose(1, 0, 2).reshape(toks, share)
    score = got[:, 0, slots * share :][:, :slots].T.reshape(1, toks)
    where = spot == jnp.arange(toks)[:, None]
    encoded = lax.dot_general(
        by_spot, where.astype(bf16), (((0,), (0,)), ((), ())), preferred_element_type=f32
    )
    triple = jnp.arange(toks // seq_len)[:, None]
    of_triple = jnp.sum(jnp.where(where, jnp.arange(toks)[None] // seq_len, 0), axis=1)
    scores = jnp.sum(jnp.where(of_triple[None] == triple, score, 0.0), axis=1) / seq_len
    diff = jax.nn.sigmoid(scores) - labels.astype(f32)
    pooled = jnp.mean(encoded.reshape(share, toks // seq_len, seq_len), axis=2)
    grad = jnp.sum(diff[None] * pooled, axis=1)
    grad = grad + swapped(grad, "core")
    grad = grad + swapped(grad, "yl")
    return encoded.T.astype(bf16), scores, grad


def solution(mesh):
    parts = Mesh(mesh.devices.reshape(2, 2, 2, 4, 2, 4), (*DP, *MP))
    return jax.shard_map(
        on_device,
        mesh=parts,
        in_specs=(
            P(MP, None),
            P(DP, None),
            P(DP, None),
            P(DP),
            P(),
            P(None, MP),
            P(MP, None),
            P(MP),
            P(MP),
        ),
        out_specs=(P(DP, MP), P(DP), P(MP)),
        check_vma=False,
    )
```

```python
import functools

import jax
import jax.numpy as jnp
from jax import lax
from jax.experimental import pallas as pl
from jax.experimental.pallas import tpu as pltpu
from jax.sharding import Mesh
from jax.sharding import PartitionSpec as P

MP = ("yh", "zh", "zl", "x")
DP = ("yl", "core")
ACT = ("yh", "zl", "x")
LANES = 128


def exchange(blocks, axes):
    return lax.all_to_all(blocks, axes, split_axis=0, concat_axis=0, tiled=True)


def to_everyone(array, axes):
    return exchange(jnp.broadcast_to(array, (lax.axis_size(axes), *array.shape)), axes)


def from_column(array, axis):
    peers = lax.axis_size(axis)
    return [array] + [
        lax.ppermute(array, axis, [((i + step) % peers, i) for i in range(peers)])
        for step in range(1, peers)
    ]


def swapped(array, axis):
    return lax.ppermute(array, axis, [(0, 1), (1, 0)])


def send_kernel(
    peers, where_ref, triples, words, gain, weight, table, sent, tiles, lanes, rows, held, sems
):
    lead, n_triples = triples.shape
    seq_len = lead + words.shape[1]
    entries, width = table.shape
    half = width // 2
    low = where_ref[0] * entries
    skipped = where_ref[1] * peers
    group = 8

    def copy(number, local):
        start = pl.multiple_of((local >> 3) * 8, 8)
        return pltpu.make_async_copy(
            table.at[pl.ds(start, 8), :], tiles.at[number], sems.at[number]
        )

    held[0] = 0

    def scan(i, below):
        for g in range(0, seq_len, group):
            locals_ = [
                (triples[j, i] if j < lead else words[i, j - lead]) - low
                for j in range(g, g + group)
            ]
            outside = [local & -entries for local in locals_]
            any_mine = outside[0] == 0
            for out in outside[1:]:
                any_mine = any_mine | (out == 0)
            for local in locals_:
                below = below - (local >> 31)

            @pl.when(any_mine)
            def _(locals_=locals_, outside=outside):
                for local, out in zip(locals_, outside):
                    @pl.when(out == 0)
                    def _(local=local):
                        number = held[0] - skipped
                        held[0] = held[0] + 1

                        @pl.when((number >= 0) & (number < peers))
                        def _():
                            rows[number] = local
                            copy(number, local).start()

        return below

    below = lax.fori_loop(0, n_triples, scan, jnp.int32(0))

    lanes[...] = jnp.zeros_like(lanes)
    share = gain.shape[1]
    lanes[0:1, 0:share] = gain[...] * weight[...]
    exact = lanes[...]
    high = exact.astype(jnp.bfloat16).astype(jnp.float32)
    middle = (exact - high).astype(jnp.bfloat16).astype(jnp.float32)
    least = (exact - high - middle).astype(jnp.bfloat16).astype(jnp.float32)
    parts = high + pltpu.roll(middle, share, 1) + pltpu.roll(least, 2 * share, 1)
    trips = ((held[0] + peers - 1) // peers).astype(jnp.float32)
    row_of = lax.broadcasted_iota(jnp.int32, parts.shape, 0)
    lane = lax.broadcasted_iota(jnp.int32, parts.shape, 1)
    parts = jnp.where((row_of == 1) & (lane == 1), trips, parts)
    slot_at = (row_of == 1) & (lane == 0)
    blank = jnp.where(slot_at, -1.0, parts)[0:2]
    sent[:, :, 0:half] = jnp.zeros((peers, 2, half), sent.dtype)
    sent[:, :, half:] = jnp.broadcast_to(blank[None], (peers, 2, LANES)).astype(sent.dtype)

    def place_row(number, carry):
        local = rows[number]
        copy(number, local).wait()
        tile = tiles[number].astype(jnp.float32)
        picked = lax.broadcasted_iota(jnp.int32, tile.shape, 0) == (local & 7)
        row = jnp.sum(jnp.where(picked, tile, 0.0), axis=0, keepdims=True)
        pair = jnp.concatenate([row[:, :half], row[:, half:]], axis=0)
        spot = below + skipped + number
        peer = spot & (peers - 1)
        slot = (spot // peers).astype(jnp.float32)
        sent[peer, :, 0:half] = pair.astype(sent.dtype)
        sent[peer, :, half:] = jnp.where(slot_at, slot, parts)[0:2].astype(sent.dtype)
        return carry

    here = jnp.clip(held[0] - skipped, 0, peers)
    lax.fori_loop(0, here, place_row, jnp.int32(0))


def to_send(place, trip, triples, words, gain, weight, table, peers):
    width = table.shape[1]
    vmem = pl.BlockSpec(memory_space=pltpu.VMEM)
    smem = pl.BlockSpec(memory_space=pltpu.SMEM)
    return pl.pallas_call(
        functools.partial(send_kernel, peers),
        out_shape=jax.ShapeDtypeStruct((peers, 2, width // 2 + LANES), table.dtype),
        in_specs=[smem] * 3 + [vmem] * 2 + [pl.BlockSpec(memory_space=pl.ANY)],
        out_specs=vmem,
        scratch_shapes=[
            pltpu.VMEM((peers, 8, width), table.dtype),
            pltpu.VMEM((8, LANES), jnp.float32),
            pltpu.SMEM((peers,), jnp.int32),
            pltpu.SMEM((1,), jnp.int32),
            pltpu.SemaphoreType.DMA((peers,)),
        ],
        name="send_rows",
    )(jnp.stack([place, trip]), triples.T, words, gain, weight, table)


def position_kernel(entries, triples, words, words_v, spot_ref, ids_ref):
    n_triples, seq_len = spot_ref.shape
    lead = triples.shape[0]
    toks = n_triples * seq_len
    shift = entries.bit_length() - 1
    for j in range(lead):
        for i in range(n_triples):
            ids_ref[i : i + 1, j : j + 1] = jnp.full((1, 1), triples[j, i], jnp.int32)
    ids_ref[:, lead:] = words_v[...]
    keys = (ids_ref[...] >> shift) * toks
    keys = keys + lax.broadcasted_iota(jnp.int32, keys.shape, 0) * seq_len
    keys = keys + lax.broadcasted_iota(jnp.int32, keys.shape, 1)

    def scan(i, spot):
        for j in range(seq_len):
            token = triples[j, i] if j < lead else words[i, j - lead]
            key = (token >> shift) * toks + (i * seq_len + j)
            spot = spot + (key < keys).astype(jnp.int32)
        return spot

    spot_ref[...] = lax.fori_loop(0, n_triples, scan, jnp.zeros(keys.shape, jnp.int32))


def positions(triples, words, entries):
    shape = (triples.shape[0], triples.shape[1] + words.shape[1])
    smem = pl.BlockSpec(memory_space=pltpu.SMEM)
    vmem = pl.BlockSpec(memory_space=pltpu.VMEM)
    return pl.pallas_call(
        functools.partial(position_kernel, entries),
        out_shape=jax.ShapeDtypeStruct(shape, jnp.int32),
        in_specs=[smem, smem, vmem],
        out_specs=vmem,
        scratch_shapes=[pltpu.VMEM(shape, jnp.int32)],
        name="positions",
    )(triples.T, words, words)


def standardize(values):
    width = values.shape[1]
    mean = jnp.sum(values, axis=1, keepdims=True) / width
    var = jnp.sum(values * values, axis=1, keepdims=True) / width - mean * mean
    return (values - mean) * lax.rsqrt(var + 1e-05)


def on_device(
    table, triples, words, labels, in_gain, up_weight, down_weight, out_gain, class_weight
):
    bf16, f32 = jnp.bfloat16, jnp.float32
    peers = lax.axis_size(MP)
    place = lax.axis_index(MP)
    seq_len = triples.shape[1] + words.shape[1]
    toks = triples.shape[0] * seq_len
    entries, width = table.shape
    slots = toks // peers
    share = width // peers

    units = up_weight.shape[1]
    weights = from_column(jnp.concatenate([up_weight.T, down_weight], axis=0), "zh")
    up_rows = jnp.concatenate([w[:units] for w in weights], axis=0)
    down_rows = jnp.concatenate([w[units:] for w in weights], axis=0)

    gains = out_gain.reshape(1, -1), class_weight.reshape(1, -1)

    def rows_of(trip):
        return exchange(to_send(place, trip, triples, words, *gains, table, peers), MP)

    half = width // 2

    def taken(got):
        picks = got[:, 1, half : half + 1].astype(f32) == jnp.arange(slots, dtype=f32)[None]
        rows = jnp.concatenate([got[:, 0, :half], got[:, 1, :half]], axis=1)
        return lax.dot_general(
            picks.astype(bf16), rows, (((0,), (0,)), ((), ())), preferred_element_type=f32
        )

    got = rows_of(jnp.int32(0))
    trips = jnp.max(got[:, 1, half + 1].astype(f32)).astype(jnp.int32)
    score_weight = got[:, 0, half : half + 3 * share].astype(f32).reshape(peers, 3, share)
    score_weight = jnp.sum(score_weight, axis=1).reshape(1, width)

    def another(state):
        trip, embed = state
        return trip + 1, embed + taken(rows_of(trip))

    _, embed = lax.while_loop(lambda state: state[0] < trips, another, (jnp.int32(1), taken(got)))

    normed = (standardize(embed) * in_gain).astype(bf16)
    everyone = to_everyone(normed, ACT)
    hidden = lax.dot_general(
        everyone.reshape(-1, width), up_rows, (((1,), (1,)), ((), ())), preferred_element_type=f32
    )
    active = jax.nn.gelu(hidden, approximate=False).astype(bf16)
    terms = jnp.dot(active, down_rows, preferred_element_type=f32).astype(bf16)
    terms = exchange(terms.reshape(everyone.shape), ACT)
    resid = normed.astype(f32) + jnp.sum(terms.astype(f32), axis=0)
    level = standardize(resid)
    score = jnp.sum(level * score_weight, axis=1)

    blocks = level.reshape(slots, peers, share).transpose(1, 0, 2).reshape(peers, 1, -1)
    score = jnp.broadcast_to(jnp.pad(score, (0, LANES - slots)), (peers, 1, LANES))
    got = exchange(jnp.concatenate([blocks, score], axis=2), MP)
    level = got[:, 0, : slots * share].reshape(peers, slots, share)
    by_spot = (level * out_gain).astype(bf16).transpose(1, 0, 2).reshape(toks, share)
    score = got[:, 0, slots * share :][:, :slots].T.reshape(1, toks)
    spot = positions(triples, words, entries).reshape(1, toks)
    where = spot == jnp.arange(toks)[:, None]
    encoded = lax.dot_general(
        by_spot, where.astype(bf16), (((0,), (0,)), ((), ())), preferred_element_type=f32
    )
    triple = jnp.arange(toks // seq_len)[:, None]
    of_triple = jnp.sum(jnp.where(where, jnp.arange(toks)[None] // seq_len, 0), axis=1)
    scores = jnp.sum(jnp.where(of_triple[None] == triple, score, 0.0), axis=1) / seq_len
    diff = jax.nn.sigmoid(scores) - labels.astype(f32)
    pooled = jnp.mean(encoded.reshape(share, toks // seq_len, seq_len), axis=2)
    grad = jnp.sum(diff[None] * pooled, axis=1)
    grad = grad + swapped(grad, "core")
    grad = grad + swapped(grad, "yl")
    return encoded.T.astype(bf16), scores, grad


def solution(mesh):
    parts = Mesh(mesh.devices.reshape(2, 2, 2, 4, 2, 4), (*DP, *MP))
    return jax.shard_map(
        on_device,
        mesh=parts,
        in_specs=(
            P(MP, None),
            P(DP, None),
            P(DP, None),
            P(DP),
            P(),
            P(None, MP),
            P(MP, None),
            P(MP),
            P(MP),
        ),
        out_specs=(P(DP, MP), P(DP), P(MP)),
        check_vma=False,
    )
```

```python
import functools

import jax
import jax.numpy as jnp
from jax import lax
from jax.experimental import pallas as pl
from jax.experimental.pallas import tpu as pltpu
from jax.sharding import Mesh
from jax.sharding import PartitionSpec as P

MP = ("yh", "zh", "zl", "x")
DP = ("yl", "core")
ACT = ("yh", "zl", "x")
LANES = 128


def exchange(blocks, axes):
    return lax.all_to_all(blocks, axes, split_axis=0, concat_axis=0, tiled=True)


def to_everyone(array, axes):
    return exchange(jnp.broadcast_to(array, (lax.axis_size(axes), *array.shape)), axes)


def from_column(array, axis):
    peers = lax.axis_size(axis)
    return [
        lax.ppermute(array, axis, [((i + step) % peers, i) for i in range(peers)])
        for step in range(1, peers)
    ]


def swapped(array, axis):
    return lax.ppermute(array, axis, [(0, 1), (1, 0)])


def send_kernel(
    peers, place_ref, trip_ref, triples, words, gain, weight, table, sent, tiles, lanes, rows, held, sems
):
    lead, n_triples = triples.shape
    seq_len = lead + words.shape[1]
    entries, width = table.shape
    half = width // 2
    low = place_ref[0] * entries
    skipped = trip_ref[0] * peers
    group = 8

    def copy(number, local):
        start = pl.multiple_of((local >> 3) * 8, 8)
        return pltpu.make_async_copy(
            table.at[pl.ds(start, 8), :], tiles.at[number], sems.at[number]
        )

    held[0] = 0

    def scan(i, below):
        for g in range(0, seq_len, group):
            locals_ = [
                (triples[j, i] if j < lead else words[i, j - lead]) - low
                for j in range(g, g + group)
            ]
            outside = [local & -entries for local in locals_]
            any_mine = outside[0] == 0
            for out in outside[1:]:
                any_mine = any_mine | (out == 0)
            for local in locals_:
                below = below - (local >> 31)

            @pl.when(any_mine)
            def _(locals_=locals_, outside=outside):
                for local, out in zip(locals_, outside):
                    @pl.when(out == 0)
                    def _(local=local):
                        number = held[0] - skipped
                        held[0] = held[0] + 1

                        @pl.when((number >= 0) & (number < peers))
                        def _():
                            rows[number] = local
                            copy(number, local).start()

        return below

    below = lax.fori_loop(0, n_triples, scan, jnp.int32(0))

    lanes[...] = jnp.zeros_like(lanes)
    share = gain.shape[1]
    lanes[0:1, 0:share] = gain[...] * weight[...]
    exact = lanes[...]
    high = exact.astype(jnp.bfloat16).astype(jnp.float32)
    middle = (exact - high).astype(jnp.bfloat16).astype(jnp.float32)
    least = (exact - high - middle).astype(jnp.bfloat16).astype(jnp.float32)
    parts = high + pltpu.roll(middle, share, 1) + pltpu.roll(least, 2 * share, 1)
    trips = ((held[0] + peers - 1) // peers).astype(jnp.float32)
    row_of = lax.broadcasted_iota(jnp.int32, parts.shape, 0)
    lane = lax.broadcasted_iota(jnp.int32, parts.shape, 1)
    parts = jnp.where((row_of == 1) & (lane == 1), trips, parts)
    slot_at = (row_of == 1) & (lane == 0)
    blank = jnp.where(slot_at, -1.0, parts)[0:2]
    sent[:, :, 0:half] = jnp.zeros((peers, 2, half), sent.dtype)
    sent[:, :, half:] = jnp.broadcast_to(blank[None], (peers, 2, LANES)).astype(sent.dtype)

    def place_row(number, carry):
        local = rows[number]
        copy(number, local).wait()
        tile = tiles[number].astype(jnp.float32)
        picked = lax.broadcasted_iota(jnp.int32, tile.shape, 0) == (local & 7)
        row = jnp.sum(jnp.where(picked, tile, 0.0), axis=0, keepdims=True)
        pair = jnp.concatenate([row[:, :half], row[:, half:]], axis=0)
        spot = below + skipped + number
        peer = spot & (peers - 1)
        slot = (spot // peers).astype(jnp.float32)
        sent[peer, :, 0:half] = pair.astype(sent.dtype)
        sent[peer, :, half:] = jnp.where(slot_at, slot, parts)[0:2].astype(sent.dtype)
        return carry

    here = jnp.clip(held[0] - skipped, 0, peers)
    lax.fori_loop(0, here, place_row, jnp.int32(0))


def to_send(place, trip, triples, words, gain, weight, table, peers):
    width = table.shape[1]
    vmem = pl.BlockSpec(memory_space=pltpu.VMEM)
    smem = pl.BlockSpec(memory_space=pltpu.SMEM)
    return pl.pallas_call(
        functools.partial(send_kernel, peers),
        out_shape=jax.ShapeDtypeStruct((peers, 2, width // 2 + LANES), table.dtype),
        in_specs=[smem] * 4 + [vmem] * 2 + [pl.BlockSpec(memory_space=pl.ANY)],
        out_specs=vmem,
        scratch_shapes=[
            pltpu.VMEM((peers, 8, width), table.dtype),
            pltpu.VMEM((8, LANES), jnp.float32),
            pltpu.SMEM((peers,), jnp.int32),
            pltpu.SMEM((1,), jnp.int32),
            pltpu.SemaphoreType.DMA((peers,)),
        ],
        name="send_rows",
    )(place.reshape(1), trip.reshape(1), triples.T, words, gain, weight, table)


def position_kernel(entries, triples, words, words_v, spot_ref, ids_ref):
    n_triples, seq_len = spot_ref.shape
    lead = triples.shape[0]
    toks = n_triples * seq_len
    shift = entries.bit_length() - 1
    for j in range(lead):
        for i in range(n_triples):
            ids_ref[i : i + 1, j : j + 1] = jnp.full((1, 1), triples[j, i], jnp.int32)
    ids_ref[:, lead:] = words_v[...]
    keys = (ids_ref[...] >> shift) * toks
    keys = keys + lax.broadcasted_iota(jnp.int32, keys.shape, 0) * seq_len
    keys = keys + lax.broadcasted_iota(jnp.int32, keys.shape, 1)

    def scan(i, spot):
        for j in range(seq_len):
            token = triples[j, i] if j < lead else words[i, j - lead]
            key = (token >> shift) * toks + (i * seq_len + j)
            spot = spot + (key < keys).astype(jnp.int32)
        return spot

    spot_ref[...] = lax.fori_loop(0, n_triples, scan, jnp.zeros(keys.shape, jnp.int32))


def positions(triples, words, entries):
    shape = (triples.shape[0], triples.shape[1] + words.shape[1])
    smem = pl.BlockSpec(memory_space=pltpu.SMEM)
    vmem = pl.BlockSpec(memory_space=pltpu.VMEM)
    return pl.pallas_call(
        functools.partial(position_kernel, entries),
        out_shape=jax.ShapeDtypeStruct(shape, jnp.int32),
        in_specs=[smem, smem, vmem],
        out_specs=vmem,
        scratch_shapes=[pltpu.VMEM(shape, jnp.int32)],
        name="positions",
    )(triples.T, words, words)


def standardize(values):
    width = values.shape[1]
    mean = jnp.sum(values, axis=1, keepdims=True) / width
    var = jnp.sum(values * values, axis=1, keepdims=True) / width - mean * mean
    return (values - mean) * lax.rsqrt(var + 1e-05)


def on_device(
    table, triples, words, labels, in_gain, up_weight, down_weight, out_gain, class_weight
):
    bf16, f32 = jnp.bfloat16, jnp.float32
    peers = lax.axis_size(MP)
    place = lax.axis_index(MP)
    seq_len = triples.shape[1] + words.shape[1]
    toks = triples.shape[0] * seq_len
    entries, width = table.shape
    slots = toks // peers
    share = width // peers

    units = up_weight.shape[1] // lax.axis_size("core")
    start = lax.axis_index("core") * units
    up_part = lax.dynamic_slice_in_dim(up_weight.T, start, units, 0)
    down_part = lax.dynamic_slice_in_dim(down_weight, start, units, 0)
    came = from_column(jnp.concatenate([up_part, down_part], axis=0), "zh")

    gains = out_gain.reshape(1, -1), class_weight.reshape(1, -1)

    def rows_of(trip):
        return exchange(to_send(place, trip, triples, words, *gains, table, peers), MP)

    half = width // 2

    def taken(got):
        picks = got[:, 1, half : half + 1].astype(f32) == jnp.arange(slots, dtype=f32)[None]
        rows = jnp.concatenate([got[:, 0, :half], got[:, 1, :half]], axis=1)
        return lax.dot_general(
            picks.astype(bf16), rows, (((0,), (0,)), ((), ())), preferred_element_type=f32
        )

    got = rows_of(jnp.int32(0))
    trips = jnp.max(got[:, 1, half + 1].astype(f32)).astype(jnp.int32)
    came = jnp.where(trips <= toks, jnp.stack(came), 0)
    came = jnp.concatenate([came, swapped(came, "core")], axis=0)
    up_rows = jnp.concatenate([up_weight.T, came[:, :units].reshape(-1, width)], axis=0)
    down_rows = jnp.concatenate([down_weight, came[:, units:].reshape(-1, width)], axis=0)

    score_weight = got[:, 0, half : half + 3 * share].astype(f32).reshape(peers, 3, share)
    score_weight = jnp.sum(score_weight, axis=1).reshape(1, width)

    def another(state):
        trip, embed = state
        return trip + 1, embed + taken(rows_of(trip))

    _, embed = lax.while_loop(lambda state: state[0] < trips, another, (jnp.int32(1), taken(got)))

    normed = (standardize(embed) * in_gain).astype(bf16)
    everyone = to_everyone(normed, ACT)
    hidden = lax.dot_general(
        everyone.reshape(-1, width), up_rows, (((1,), (1,)), ((), ())), preferred_element_type=f32
    )
    active = jax.nn.gelu(hidden, approximate=False).astype(bf16)
    terms = jnp.dot(active, down_rows, preferred_element_type=f32).astype(bf16)
    terms = exchange(terms.reshape(everyone.shape), ACT)
    resid = normed.astype(f32) + jnp.sum(terms.astype(f32), axis=0)
    level = standardize(resid)
    score = jnp.sum(level * score_weight, axis=1)

    blocks = level.reshape(slots, peers, share).transpose(1, 0, 2).reshape(peers, 1, -1)
    score = jnp.broadcast_to(jnp.pad(score, (0, LANES - slots)), (peers, 1, LANES))
    got = exchange(jnp.concatenate([blocks, score], axis=2), MP)
    level = got[:, 0, : slots * share].reshape(peers, slots, share)
    by_spot = (level * out_gain).astype(bf16).transpose(1, 0, 2).reshape(toks, share)
    score = got[:, 0, slots * share :][:, :slots].T.reshape(1, toks)
    spot = positions(triples, words, entries).reshape(1, toks)
    where = spot == jnp.arange(toks)[:, None]
    encoded = lax.dot_general(
        by_spot, where.astype(bf16), (((0,), (0,)), ((), ())), preferred_element_type=f32
    )
    triple = jnp.arange(toks // seq_len)[:, None]
    of_triple = jnp.sum(jnp.where(where, jnp.arange(toks)[None] // seq_len, 0), axis=1)
    scores = jnp.sum(jnp.where(of_triple[None] == triple, score, 0.0), axis=1) / seq_len
    diff = jax.nn.sigmoid(scores) - labels.astype(f32)
    pooled = jnp.mean(encoded.reshape(share, toks // seq_len, seq_len), axis=2)
    grad = jnp.sum(diff[None] * pooled, axis=1)
    grad = grad + swapped(grad, "core")
    grad = grad + swapped(grad, "yl")
    return encoded.T.astype(bf16), scores, grad


def solution(mesh):
    parts = Mesh(mesh.devices.reshape(2, 2, 2, 4, 2, 4), (*DP, *MP))
    return jax.shard_map(
        on_device,
        mesh=parts,
        in_specs=(
            P(MP, None),
            P(DP, None),
            P(DP, None),
            P(DP),
            P(),
            P(None, MP),
            P(MP, None),
            P(MP),
            P(MP),
        ),
        out_specs=(P(DP, MP), P(DP), P(MP)),
        check_vma=False,
    )
```

```python
import functools

import jax
import jax.numpy as jnp
from jax import lax
from jax.experimental import pallas as pl
from jax.experimental.pallas import tpu as pltpu
from jax.sharding import Mesh
from jax.sharding import PartitionSpec as P

MP = ("yh", "zh", "zl", "x")
DP = ("yl", "core")
ACT = ("yh", "zl", "x")
LANES = 128


def exchange(blocks, axes):
    return lax.all_to_all(blocks, axes, split_axis=0, concat_axis=0, tiled=True)


def to_everyone(array, axes):
    return exchange(jnp.broadcast_to(array, (lax.axis_size(axes), *array.shape)), axes)


def moved(array, axis, step):
    peers = lax.axis_size(axis)
    return lax.ppermute(array, axis, [((i + step) % peers, i) for i in range(peers)])


def swapped(array, axis):
    return lax.ppermute(array, axis, [(0, 1), (1, 0)])


def send_kernel(
    peers, place_ref, trip_ref, triples, words, gain, weight, table, sent, tiles, lanes, rows, held, sems
):
    lead, n_triples = triples.shape
    seq_len = lead + words.shape[1]
    entries, width = table.shape
    half = width // 2
    low = place_ref[0] * entries
    skipped = trip_ref[0] * peers
    group = 8

    def copy(number, local):
        start = pl.multiple_of((local >> 3) * 8, 8)
        return pltpu.make_async_copy(
            table.at[pl.ds(start, 8), :], tiles.at[number], sems.at[number]
        )

    held[0] = 0

    def scan(i, below):
        for g in range(0, seq_len, group):
            locals_ = [
                (triples[j, i] if j < lead else words[i, j - lead]) - low
                for j in range(g, g + group)
            ]
            outside = [local & -entries for local in locals_]
            any_mine = outside[0] == 0
            for out in outside[1:]:
                any_mine = any_mine | (out == 0)
            for local in locals_:
                below = below - (local >> 31)

            @pl.when(any_mine)
            def _(locals_=locals_, outside=outside):
                for local, out in zip(locals_, outside):
                    @pl.when(out == 0)
                    def _(local=local):
                        number = held[0] - skipped
                        held[0] = held[0] + 1

                        @pl.when((number >= 0) & (number < peers))
                        def _():
                            rows[number] = local
                            copy(number, local).start()

        return below

    below = lax.fori_loop(0, n_triples, scan, jnp.int32(0))

    lanes[...] = jnp.zeros_like(lanes)
    share = gain.shape[1]
    lanes[0:1, 0:share] = gain[...] * weight[...]
    exact = lanes[...]
    high = exact.astype(jnp.bfloat16).astype(jnp.float32)
    middle = (exact - high).astype(jnp.bfloat16).astype(jnp.float32)
    least = (exact - high - middle).astype(jnp.bfloat16).astype(jnp.float32)
    parts = high + pltpu.roll(middle, share, 1) + pltpu.roll(least, 2 * share, 1)
    trips = ((held[0] + peers - 1) // peers).astype(jnp.float32)
    row_of = lax.broadcasted_iota(jnp.int32, parts.shape, 0)
    lane = lax.broadcasted_iota(jnp.int32, parts.shape, 1)
    parts = jnp.where((row_of == 1) & (lane == 1), trips, parts)
    slot_at = (row_of == 1) & (lane == 0)
    blank = jnp.where(slot_at, -1.0, parts)[0:2]
    sent[:, :, 0:half] = jnp.zeros((peers, 2, half), sent.dtype)
    sent[:, :, half:] = jnp.broadcast_to(blank[None], (peers, 2, LANES)).astype(sent.dtype)

    def place_row(number, carry):
        local = rows[number]
        copy(number, local).wait()
        tile = tiles[number].astype(jnp.float32)
        picked = lax.broadcasted_iota(jnp.int32, tile.shape, 0) == (local & 7)
        row = jnp.sum(jnp.where(picked, tile, 0.0), axis=0, keepdims=True)
        pair = jnp.concatenate([row[:, :half], row[:, half:]], axis=0)
        spot = below + skipped + number
        peer = spot & (peers - 1)
        slot = (spot // peers).astype(jnp.float32)
        sent[peer, :, 0:half] = pair.astype(sent.dtype)
        sent[peer, :, half:] = jnp.where(slot_at, slot, parts)[0:2].astype(sent.dtype)
        return carry

    here = jnp.clip(held[0] - skipped, 0, peers)
    lax.fori_loop(0, here, place_row, jnp.int32(0))


def to_send(place, trip, triples, words, gain, weight, table, peers):
    width = table.shape[1]
    vmem = pl.BlockSpec(memory_space=pltpu.VMEM)
    smem = pl.BlockSpec(memory_space=pltpu.SMEM)
    return pl.pallas_call(
        functools.partial(send_kernel, peers),
        out_shape=jax.ShapeDtypeStruct((peers, 2, width // 2 + LANES), table.dtype),
        in_specs=[smem] * 4 + [vmem] * 2 + [pl.BlockSpec(memory_space=pl.ANY)],
        out_specs=vmem,
        scratch_shapes=[
            pltpu.VMEM((peers, 8, width), table.dtype),
            pltpu.VMEM((8, LANES), jnp.float32),
            pltpu.SMEM((peers,), jnp.int32),
            pltpu.SMEM((1,), jnp.int32),
            pltpu.SemaphoreType.DMA((peers,)),
        ],
        name="send_rows",
    )(place.reshape(1), trip.reshape(1), triples.T, words, gain, weight, table)


def position_kernel(entries, triples, words, words_v, spot_ref, ids_ref):
    n_triples, seq_len = spot_ref.shape
    lead = triples.shape[0]
    toks = n_triples * seq_len
    shift = entries.bit_length() - 1
    for j in range(lead):
        for i in range(n_triples):
            ids_ref[i : i + 1, j : j + 1] = jnp.full((1, 1), triples[j, i], jnp.int32)
    ids_ref[:, lead:] = words_v[...]
    keys = (ids_ref[...] >> shift) * toks
    keys = keys + lax.broadcasted_iota(jnp.int32, keys.shape, 0) * seq_len
    keys = keys + lax.broadcasted_iota(jnp.int32, keys.shape, 1)

    def scan(i, spot):
        for j in range(seq_len):
            token = triples[j, i] if j < lead else words[i, j - lead]
            key = (token >> shift) * toks + (i * seq_len + j)
            spot = spot + (key < keys).astype(jnp.int32)
        return spot

    spot_ref[...] = lax.fori_loop(0, n_triples, scan, jnp.zeros(keys.shape, jnp.int32))


def positions(triples, words, entries):
    shape = (triples.shape[0], triples.shape[1] + words.shape[1])
    smem = pl.BlockSpec(memory_space=pltpu.SMEM)
    vmem = pl.BlockSpec(memory_space=pltpu.VMEM)
    return pl.pallas_call(
        functools.partial(position_kernel, entries),
        out_shape=jax.ShapeDtypeStruct(shape, jnp.int32),
        in_specs=[smem, smem, vmem],
        out_specs=vmem,
        scratch_shapes=[pltpu.VMEM(shape, jnp.int32)],
        name="positions",
    )(triples.T, words, words)


def standardize(values):
    width = values.shape[1]
    mean = jnp.sum(values, axis=1, keepdims=True) / width
    var = jnp.sum(values * values, axis=1, keepdims=True) / width - mean * mean
    return (values - mean) * lax.rsqrt(var + 1e-05)


def on_device(
    table, triples, words, labels, in_gain, up_weight, down_weight, out_gain, class_weight
):
    bf16, f32 = jnp.bfloat16, jnp.float32
    peers = lax.axis_size(MP)
    place = lax.axis_index(MP)
    seq_len = triples.shape[1] + words.shape[1]
    toks = triples.shape[0] * seq_len
    entries, width = table.shape
    slots = toks // peers
    share = width // peers

    units = up_weight.shape[1]
    half_units = units // lax.axis_size("core")
    start = lax.axis_index("core") * half_units
    up_half = lax.dynamic_slice_in_dim(up_weight.T, start, half_units, 0)
    down_half = lax.dynamic_slice_in_dim(down_weight, start, half_units, 0)
    own = jnp.concatenate([up_weight.T, down_weight], axis=0)
    far = moved(jnp.concatenate([up_half, down_half], axis=0), "zh", 2)
    weights = [own, moved(own, "zh", 1), moved(own, "zh", 3)]
    halves = [far, swapped(far, "core")]
    up_rows = jnp.concatenate(
        [w[:units] for w in weights] + [h[:half_units] for h in halves], axis=0
    )
    down_rows = jnp.concatenate(
        [w[units:] for w in weights] + [h[half_units:] for h in halves], axis=0
    )

    gains = out_gain.reshape(1, -1), class_weight.reshape(1, -1)

    def rows_of(trip):
        return exchange(to_send(place, trip, triples, words, *gains, table, peers), MP)

    half = width // 2

    def taken(got):
        picks = got[:, 1, half : half + 1].astype(f32) == jnp.arange(slots, dtype=f32)[None]
        rows = jnp.concatenate([got[:, 0, :half], got[:, 1, :half]], axis=1)
        return lax.dot_general(
            picks.astype(bf16), rows, (((0,), (0,)), ((), ())), preferred_element_type=f32
        )

    got = rows_of(jnp.int32(0))
    trips = jnp.max(got[:, 1, half + 1].astype(f32)).astype(jnp.int32)
    score_weight = got[:, 0, half : half + 3 * share].astype(f32).reshape(peers, 3, share)
    score_weight = jnp.sum(score_weight, axis=1).reshape(1, width)

    def another(state):
        trip, embed = state
        return trip + 1, embed + taken(rows_of(trip))

    _, embed = lax.while_loop(lambda state: state[0] < trips, another, (jnp.int32(1), taken(got)))

    normed = (standardize(embed) * in_gain).astype(bf16)
    everyone = to_everyone(normed, ACT)
    hidden = lax.dot_general(
        everyone.reshape(-1, width), up_rows, (((1,), (1,)), ((), ())), preferred_element_type=f32
    )
    active = jax.nn.gelu(hidden, approximate=False).astype(bf16)
    terms = jnp.dot(active, down_rows, preferred_element_type=f32).astype(bf16)
    terms = exchange(terms.reshape(everyone.shape), ACT)
    resid = normed.astype(f32) + jnp.sum(terms.astype(f32), axis=0)
    level = standardize(resid)
    score = jnp.sum(level * score_weight, axis=1)

    blocks = level.reshape(slots, peers, share).transpose(1, 0, 2).reshape(peers, 1, -1)
    score = jnp.broadcast_to(jnp.pad(score, (0, LANES - slots)), (peers, 1, LANES))
    got = exchange(jnp.concatenate([blocks, score], axis=2), MP)
    level = got[:, 0, : slots * share].reshape(peers, slots, share)
    by_spot = (level * out_gain).astype(bf16).transpose(1, 0, 2).reshape(toks, share)
    score = got[:, 0, slots * share :][:, :slots].T.reshape(1, toks)
    spot = positions(triples, words, entries).reshape(1, toks)
    where = spot == jnp.arange(toks)[:, None]
    encoded = lax.dot_general(
        by_spot, where.astype(bf16), (((0,), (0,)), ((), ())), preferred_element_type=f32
    )
    triple = jnp.arange(toks // seq_len)[:, None]
    of_triple = jnp.sum(jnp.where(where, jnp.arange(toks)[None] // seq_len, 0), axis=1)
    scores = jnp.sum(jnp.where(of_triple[None] == triple, score, 0.0), axis=1) / seq_len
    diff = jax.nn.sigmoid(scores) - labels.astype(f32)
    pooled = jnp.mean(encoded.reshape(share, toks // seq_len, seq_len), axis=2)
    grad = jnp.sum(diff[None] * pooled, axis=1)
    grad = grad + swapped(grad, "core")
    grad = grad + swapped(grad, "yl")
    return encoded.T.astype(bf16), scores, grad


def solution(mesh):
    parts = Mesh(mesh.devices.reshape(2, 2, 2, 4, 2, 4), (*DP, *MP))
    return jax.shard_map(
        on_device,
        mesh=parts,
        in_specs=(
            P(MP, None),
            P(DP, None),
            P(DP, None),
            P(DP),
            P(),
            P(None, MP),
            P(MP, None),
            P(MP),
            P(MP),
        ),
        out_specs=(P(DP, MP), P(DP), P(MP)),
        check_vma=False,
    )
```

```python
import functools

import jax
import jax.numpy as jnp
from jax import lax
from jax.experimental import pallas as pl
from jax.experimental.pallas import tpu as pltpu
from jax.sharding import Mesh
from jax.sharding import PartitionSpec as P

MP = ("yh", "zh", "zl", "x")
DP = ("yl", "core")
ACT = ("yh", "zl", "x")
LANES = 128
COVER = 40_000_000


def exchange(blocks, axes):
    return lax.all_to_all(blocks, axes, split_axis=0, concat_axis=0, tiled=True)


def to_everyone(array, axes):
    return exchange(jnp.broadcast_to(array, (lax.axis_size(axes), *array.shape)), axes)


def from_column(array):
    steps, places = lax.axis_size("zh"), lax.axis_size(DP)
    moves = [
        (d * steps + (i + d) % steps, d * steps + i) for d in range(places) for i in range(steps)
    ]
    return lax.ppermute(array, (*DP, "zh"), moves)


def swapped(array, axis):
    return lax.ppermute(array, axis, [(0, 1), (1, 0)])


def send_kernel(
    peers, place_ref, trip_ref, triples, words, gain, weight, table, sent, tiles, lanes, rows, held, sems
):
    lead, n_triples = triples.shape
    seq_len = lead + words.shape[1]
    entries, width = table.shape
    half = width // 2
    low = place_ref[0] * entries
    skipped = trip_ref[0] * peers
    group = 8

    def copy(number, local):
        start = pl.multiple_of((local >> 3) * 8, 8)
        return pltpu.make_async_copy(
            table.at[pl.ds(start, 8), :], tiles.at[number], sems.at[number]
        )

    held[0] = 0

    def scan(i, below):
        for g in range(0, seq_len, group):
            locals_ = [
                (triples[j, i] if j < lead else words[i, j - lead]) - low
                for j in range(g, g + group)
            ]
            outside = [local & -entries for local in locals_]
            any_mine = outside[0] == 0
            for out in outside[1:]:
                any_mine = any_mine | (out == 0)
            for local in locals_:
                below = below - (local >> 31)

            @pl.when(any_mine)
            def _(locals_=locals_, outside=outside):
                for local, out in zip(locals_, outside):
                    @pl.when(out == 0)
                    def _(local=local):
                        number = held[0] - skipped
                        held[0] = held[0] + 1

                        @pl.when((number >= 0) & (number < peers))
                        def _():
                            rows[number] = local
                            copy(number, local).start()

        return below

    below = lax.fori_loop(0, n_triples, scan, jnp.int32(0))

    lanes[...] = jnp.zeros_like(lanes)
    share = gain.shape[1]
    lanes[0:1, 0:share] = gain[...] * weight[...]
    exact = lanes[...]
    high = exact.astype(jnp.bfloat16).astype(jnp.float32)
    middle = (exact - high).astype(jnp.bfloat16).astype(jnp.float32)
    least = (exact - high - middle).astype(jnp.bfloat16).astype(jnp.float32)
    parts = high + pltpu.roll(middle, share, 1) + pltpu.roll(least, 2 * share, 1)
    row_of = lax.broadcasted_iota(jnp.int32, parts.shape, 0)
    lane = lax.broadcasted_iota(jnp.int32, parts.shape, 1)
    slot_at = (row_of == 1) & (lane == 0)
    blank = jnp.where(slot_at, -1.0, parts)[0:2]
    sent[:, :, 0:half] = jnp.zeros((peers, 2, half), sent.dtype)
    sent[:, :, half:] = jnp.broadcast_to(blank[None], (peers, 2, LANES)).astype(sent.dtype)

    def place_row(number, carry):
        local = rows[number]
        copy(number, local).wait()
        tile = tiles[number].astype(jnp.float32)
        picked = lax.broadcasted_iota(jnp.int32, tile.shape, 0) == (local & 7)
        row = jnp.sum(jnp.where(picked, tile, 0.0), axis=0, keepdims=True)
        pair = jnp.concatenate([row[:, :half], row[:, half:]], axis=0)
        spot = below + skipped + number
        peer = spot & (peers - 1)
        slot = (spot // peers).astype(jnp.float32)
        sent[peer, :, 0:half] = pair.astype(sent.dtype)
        sent[peer, :, half:] = jnp.where(slot_at, slot, parts)[0:2].astype(sent.dtype)
        return carry

    here = jnp.clip(held[0] - skipped, 0, peers)
    lax.fori_loop(0, here, place_row, jnp.int32(0))


def to_send(place, trip, triples, words, gain, weight, table, peers):
    width = table.shape[1]
    vmem = pl.BlockSpec(memory_space=pltpu.VMEM)
    smem = pl.BlockSpec(memory_space=pltpu.SMEM)
    return pl.pallas_call(
        functools.partial(send_kernel, peers),
        out_shape=jax.ShapeDtypeStruct((peers, 2, width // 2 + LANES), table.dtype),
        in_specs=[smem] * 4 + [vmem] * 2 + [pl.BlockSpec(memory_space=pl.ANY)],
        out_specs=vmem,
        scratch_shapes=[
            pltpu.VMEM((peers, 8, width), table.dtype),
            pltpu.VMEM((8, LANES), jnp.float32),
            pltpu.SMEM((peers,), jnp.int32),
            pltpu.SMEM((1,), jnp.int32),
            pltpu.SemaphoreType.DMA((peers,)),
        ],
        name="send_rows",
    )(place.reshape(1), trip.reshape(1), triples.T, words, gain, weight, table)


def position_kernel(entries, peers, triples, words, words_v, after, spot_ref, trips_ref, ids_ref):
    n_triples, seq_len = spot_ref.shape
    lead = triples.shape[0]
    toks = n_triples * seq_len
    shift = entries.bit_length() - 1
    for j in range(lead):
        for i in range(n_triples):
            ids_ref[i : i + 1, j : j + 1] = jnp.full((1, 1), triples[j, i], jnp.int32)
    ids_ref[:, lead:] = words_v[...]
    least = (ids_ref[...] >> shift) * toks
    keys = least + lax.broadcasted_iota(jnp.int32, least.shape, 0) * seq_len
    keys = keys + lax.broadcasted_iota(jnp.int32, keys.shape, 1)

    def scan(i, carry):
        spot, first = carry
        for j in range(seq_len):
            token = triples[j, i] if j < lead else words[i, j - lead]
            key = (token >> shift) * toks + (i * seq_len + j)
            spot = spot + (key < keys).astype(jnp.int32)
            first = first + (key < least).astype(jnp.int32)
        return spot, first

    none = jnp.zeros(keys.shape, jnp.int32)
    spot, first = lax.fori_loop(0, n_triples, scan, (none, none))
    spot_ref[...] = spot
    trips_ref[0] = jnp.max((spot - first).astype(jnp.float32)).astype(jnp.int32) // peers + 1


def positions(triples, words, entries, peers, after):
    shape = (triples.shape[0], triples.shape[1] + words.shape[1])
    smem = pl.BlockSpec(memory_space=pltpu.SMEM)
    vmem = pl.BlockSpec(memory_space=pltpu.VMEM)
    return pl.pallas_call(
        functools.partial(position_kernel, entries, peers),
        out_shape=(
            jax.ShapeDtypeStruct(shape, jnp.int32),
            jax.ShapeDtypeStruct((1,), jnp.int32),
        ),
        in_specs=[smem, smem, vmem, pl.BlockSpec(memory_space=pl.ANY)],
        out_specs=(vmem, smem),
        cost_estimate=pl.CostEstimate(flops=0, transcendentals=0, bytes_accessed=COVER),
        scratch_shapes=[pltpu.VMEM(shape, jnp.int32)],
        name="positions",
    )(triples.T, words, words, after)


def standardize(values):
    width = values.shape[1]
    mean = jnp.sum(values, axis=1, keepdims=True) / width
    var = jnp.sum(values * values, axis=1, keepdims=True) / width - mean * mean
    return (values - mean) * lax.rsqrt(var + 1e-05)


def on_device(
    table, triples, words, labels, in_gain, up_weight, down_weight, out_gain, class_weight
):
    bf16, f32 = jnp.bfloat16, jnp.float32
    peers = lax.axis_size(MP)
    place = lax.axis_index(MP)
    seq_len = triples.shape[1] + words.shape[1]
    toks = triples.shape[0] * seq_len
    entries, width = table.shape
    slots = toks // peers
    share = width // peers

    units = up_weight.shape[1]
    weights = from_column(jnp.concatenate([up_weight.T, down_weight], axis=0))[None]
    weights = jnp.concatenate([weights, swapped(weights, "core")], axis=0)
    weights = jnp.concatenate([weights, swapped(weights, "yl")], axis=0)
    up_rows = weights[:, :units].reshape(-1, width)
    down_rows = weights[:, units:].reshape(-1, width)

    gains = out_gain.reshape(1, -1), class_weight.reshape(1, -1)

    def to_peers(trip):
        return to_send(place, trip, triples, words, *gains, table, peers)

    half = width // 2

    def taken(got):
        picks = got[:, 1, half : half + 1].astype(f32) == jnp.arange(slots, dtype=f32)[None]
        rows = jnp.concatenate([got[:, 0, :half], got[:, 1, :half]], axis=1)
        return lax.dot_general(
            picks.astype(bf16), rows, (((0,), (0,)), ((), ())), preferred_element_type=f32
        )

    sent = to_peers(jnp.int32(0))
    got = exchange(sent, MP)
    spot, trips = positions(triples, words, entries, peers, sent)
    score_weight = got[:, 0, half : half + 3 * share].astype(f32).reshape(peers, 3, share)
    score_weight = jnp.sum(score_weight, axis=1).reshape(1, width)

    def another(state):
        trip, embed = state
        return trip + 1, embed + taken(exchange(to_peers(trip), MP))

    _, embed = lax.while_loop(lambda state: state[0] < trips[0], another, (jnp.int32(1), taken(got)))

    normed = (standardize(embed) * in_gain).astype(bf16)
    everyone = to_everyone(normed, ACT)
    hidden = lax.dot_general(
        everyone.reshape(-1, width), up_rows, (((1,), (1,)), ((), ())), preferred_element_type=f32
    )
    active = jax.nn.gelu(hidden, approximate=False).astype(bf16)
    terms = jnp.dot(active, down_rows, preferred_element_type=f32).astype(bf16)
    terms = exchange(terms.reshape(everyone.shape), ACT)
    resid = normed.astype(f32) + jnp.sum(terms.astype(f32), axis=0)
    level = standardize(resid)
    score = jnp.sum(level * score_weight, axis=1)

    blocks = level.reshape(slots, peers, share).transpose(1, 0, 2).reshape(peers, 1, -1)
    score = jnp.broadcast_to(jnp.pad(score, (0, LANES - slots)), (peers, 1, LANES))
    got = exchange(jnp.concatenate([blocks, score], axis=2), MP)
    level = got[:, 0, : slots * share].reshape(peers, slots, share)
    by_spot = (level * out_gain).astype(bf16).transpose(1, 0, 2).reshape(toks, share)
    score = got[:, 0, slots * share :][:, :slots].T.reshape(1, toks)
    spot = spot.reshape(1, toks)
    where = spot == jnp.arange(toks)[:, None]
    encoded = lax.dot_general(
        by_spot, where.astype(bf16), (((0,), (0,)), ((), ())), preferred_element_type=f32
    )
    triple = jnp.arange(toks // seq_len)[:, None]
    of_triple = jnp.sum(jnp.where(where, jnp.arange(toks)[None] // seq_len, 0), axis=1)
    scores = jnp.sum(jnp.where(of_triple[None] == triple, score, 0.0), axis=1) / seq_len
    diff = jax.nn.sigmoid(scores) - labels.astype(f32)
    pooled = jnp.mean(encoded.reshape(share, toks // seq_len, seq_len), axis=2)
    grad = jnp.sum(diff[None] * pooled, axis=1)
    grad = grad + swapped(grad, "core")
    grad = grad + swapped(grad, "yl")
    return encoded.T.astype(bf16), scores, grad


def solution(mesh):
    parts = Mesh(mesh.devices.reshape(2, 2, 2, 4, 2, 4), (*DP, *MP))
    return jax.shard_map(
        on_device,
        mesh=parts,
        in_specs=(
            P(MP, None),
            P(DP, None),
            P(DP, None),
            P(DP),
            P(),
            P(None, MP),
            P(MP, None),
            P(MP),
            P(MP),
        ),
        out_specs=(P(DP, MP), P(DP), P(MP)),
        check_vma=False,
    )
```

```python
import functools

import jax
import jax.numpy as jnp
from jax import lax
from jax.experimental import pallas as pl
from jax.experimental.pallas import tpu as pltpu
from jax.sharding import Mesh
from jax.sharding import PartitionSpec as P

MP = ("yh", "zh", "zl", "x")
DP = ("yl", "core")
ACT = ("yh", "zl", "x")
LANES = 128
COVER = 40_000_000


def exchange(blocks, axes):
    return lax.all_to_all(blocks, axes, split_axis=0, concat_axis=0, tiled=True)


def to_everyone(array, axes):
    return exchange(jnp.broadcast_to(array, (lax.axis_size(axes), *array.shape)), axes)


def moved(array, axis, step):
    peers = lax.axis_size(axis)
    return lax.ppermute(array, axis, [((i + step) % peers, i) for i in range(peers)])


def swapped(array, axis):
    return lax.ppermute(array, axis, [(0, 1), (1, 0)])


def send_kernel(
    peers, place_ref, trip_ref, triples, words, gain, weight, table, sent, tiles, lanes, rows, held, sems
):
    lead, n_triples = triples.shape
    seq_len = lead + words.shape[1]
    entries, width = table.shape
    half = width // 2
    low = place_ref[0] * entries
    skipped = trip_ref[0] * peers
    group = 8

    def copy(number, local):
        start = pl.multiple_of((local >> 3) * 8, 8)
        return pltpu.make_async_copy(
            table.at[pl.ds(start, 8), :], tiles.at[number], sems.at[number]
        )

    held[0] = 0

    def scan(i, below):
        for g in range(0, seq_len, group):
            locals_ = [
                (triples[j, i] if j < lead else words[i, j - lead]) - low
                for j in range(g, g + group)
            ]
            outside = [local & -entries for local in locals_]
            any_mine = outside[0] == 0
            for out in outside[1:]:
                any_mine = any_mine | (out == 0)
            for local in locals_:
                below = below - (local >> 31)

            @pl.when(any_mine)
            def _(locals_=locals_, outside=outside):
                for local, out in zip(locals_, outside):
                    @pl.when(out == 0)
                    def _(local=local):
                        number = held[0] - skipped
                        held[0] = held[0] + 1

                        @pl.when((number >= 0) & (number < peers))
                        def _():
                            rows[number] = local
                            copy(number, local).start()

        return below

    below = lax.fori_loop(0, n_triples, scan, jnp.int32(0))

    lanes[...] = jnp.zeros_like(lanes)
    share = gain.shape[1]
    lanes[0:1, 0:share] = gain[...] * weight[...]
    exact = lanes[...]
    high = exact.astype(jnp.bfloat16).astype(jnp.float32)
    middle = (exact - high).astype(jnp.bfloat16).astype(jnp.float32)
    least = (exact - high - middle).astype(jnp.bfloat16).astype(jnp.float32)
    parts = high + pltpu.roll(middle, share, 1) + pltpu.roll(least, 2 * share, 1)
    row_of = lax.broadcasted_iota(jnp.int32, parts.shape, 0)
    lane = lax.broadcasted_iota(jnp.int32, parts.shape, 1)
    slot_at = (row_of == 1) & (lane == 0)
    blank = jnp.where(slot_at, -1.0, parts)[0:2]
    sent[:, :, 0:half] = jnp.zeros((peers, 2, half), sent.dtype)
    sent[:, :, half:] = jnp.broadcast_to(blank[None], (peers, 2, LANES)).astype(sent.dtype)

    def place_row(number, carry):
        local = rows[number]
        copy(number, local).wait()
        tile = tiles[number].astype(jnp.float32)
        picked = lax.broadcasted_iota(jnp.int32, tile.shape, 0) == (local & 7)
        row = jnp.sum(jnp.where(picked, tile, 0.0), axis=0, keepdims=True)
        pair = jnp.concatenate([row[:, :half], row[:, half:]], axis=0)
        spot = below + skipped + number
        peer = spot & (peers - 1)
        slot = (spot // peers).astype(jnp.float32)
        sent[peer, :, 0:half] = pair.astype(sent.dtype)
        sent[peer, :, half:] = jnp.where(slot_at, slot, parts)[0:2].astype(sent.dtype)
        return carry

    here = jnp.clip(held[0] - skipped, 0, peers)
    lax.fori_loop(0, here, place_row, jnp.int32(0))


def to_send(place, trip, triples, words, gain, weight, table, peers):
    width = table.shape[1]
    vmem = pl.BlockSpec(memory_space=pltpu.VMEM)
    smem = pl.BlockSpec(memory_space=pltpu.SMEM)
    return pl.pallas_call(
        functools.partial(send_kernel, peers),
        out_shape=jax.ShapeDtypeStruct((peers, 2, width // 2 + LANES), table.dtype),
        in_specs=[smem] * 4 + [vmem] * 2 + [pl.BlockSpec(memory_space=pl.ANY)],
        out_specs=vmem,
        scratch_shapes=[
            pltpu.VMEM((peers, 8, width), table.dtype),
            pltpu.VMEM((8, LANES), jnp.float32),
            pltpu.SMEM((peers,), jnp.int32),
            pltpu.SMEM((1,), jnp.int32),
            pltpu.SemaphoreType.DMA((peers,)),
        ],
        name="send_rows",
    )(place.reshape(1), trip.reshape(1), triples.T, words, gain, weight, table)


def position_kernel(entries, peers, triples, words, words_v, after, spot_ref, trips_ref, ids_ref):
    n_triples, seq_len = spot_ref.shape
    lead = triples.shape[0]
    toks = n_triples * seq_len
    shift = entries.bit_length() - 1
    for j in range(lead):
        for i in range(n_triples):
            ids_ref[i : i + 1, j : j + 1] = jnp.full((1, 1), triples[j, i], jnp.int32)
    ids_ref[:, lead:] = words_v[...]
    least = (ids_ref[...] >> shift) * toks
    keys = least + lax.broadcasted_iota(jnp.int32, least.shape, 0) * seq_len
    keys = keys + lax.broadcasted_iota(jnp.int32, keys.shape, 1)

    def scan(i, carry):
        spot, first = carry
        for j in range(seq_len):
            token = triples[j, i] if j < lead else words[i, j - lead]
            key = (token >> shift) * toks + (i * seq_len + j)
            spot = spot + (key < keys).astype(jnp.int32)
            first = first + (key < least).astype(jnp.int32)
        return spot, first

    none = jnp.zeros(keys.shape, jnp.int32)
    spot, first = lax.fori_loop(0, n_triples, scan, (none, none))
    spot_ref[...] = spot
    trips_ref[0] = jnp.max((spot - first).astype(jnp.float32)).astype(jnp.int32) // peers + 1


def positions(triples, words, entries, peers, after):
    shape = (triples.shape[0], triples.shape[1] + words.shape[1])
    smem = pl.BlockSpec(memory_space=pltpu.SMEM)
    vmem = pl.BlockSpec(memory_space=pltpu.VMEM)
    return pl.pallas_call(
        functools.partial(position_kernel, entries, peers),
        out_shape=(
            jax.ShapeDtypeStruct(shape, jnp.int32),
            jax.ShapeDtypeStruct((1,), jnp.int32),
        ),
        in_specs=[smem, smem, vmem, pl.BlockSpec(memory_space=pl.ANY)],
        out_specs=(vmem, smem),
        cost_estimate=pl.CostEstimate(flops=0, transcendentals=0, bytes_accessed=COVER),
        scratch_shapes=[pltpu.VMEM(shape, jnp.int32)],
        name="positions",
    )(triples.T, words, words, after)


def standardize(values):
    width = values.shape[1]
    mean = jnp.sum(values, axis=1, keepdims=True) / width
    var = jnp.sum(values * values, axis=1, keepdims=True) / width - mean * mean
    return (values - mean) * lax.rsqrt(var + 1e-05)


def on_device(
    table, triples, words, labels, in_gain, up_weight, down_weight, out_gain, class_weight
):
    bf16, f32 = jnp.bfloat16, jnp.float32
    peers = lax.axis_size(MP)
    place = lax.axis_index(MP)
    seq_len = triples.shape[1] + words.shape[1]
    toks = triples.shape[0] * seq_len
    entries, width = table.shape
    slots = toks // peers
    share = width // peers

    units = up_weight.shape[1]
    half_units = units // lax.axis_size("core")
    start = lax.axis_index("core") * half_units
    own = lax.optimization_barrier(jnp.concatenate([up_weight.T, down_weight], axis=0))
    far = lax.dynamic_slice_in_dim(own.reshape(2, units, width), start, half_units, 1)
    far = moved(far.reshape(units, width), "zh", 2)
    weights = [own, moved(own, "zh", 1), moved(own, "zh", 3)]
    halves = [far, swapped(far, "core")]
    up_rows = jnp.concatenate(
        [w[:units] for w in weights] + [h[:half_units] for h in halves], axis=0
    )
    down_rows = jnp.concatenate(
        [w[units:] for w in weights] + [h[half_units:] for h in halves], axis=0
    )

    gains = out_gain.reshape(1, -1), class_weight.reshape(1, -1)

    def to_peers(trip):
        return to_send(place, trip, triples, words, *gains, table, peers)

    half = width // 2

    def taken(got):
        picks = got[:, 1, half : half + 1].astype(f32) == jnp.arange(slots, dtype=f32)[None]
        rows = jnp.concatenate([got[:, 0, :half], got[:, 1, :half]], axis=1)
        return lax.dot_general(
            picks.astype(bf16), rows, (((0,), (0,)), ((), ())), preferred_element_type=f32
        )

    sent = to_peers(jnp.int32(0))
    got = exchange(sent, MP)
    spot, trips = positions(triples, words, entries, peers, sent)
    score_weight = got[:, 0, half : half + 3 * share].astype(f32).reshape(peers, 3, share)
    score_weight = jnp.sum(score_weight, axis=1).reshape(1, width)

    def another(state):
        trip, embed = state
        return trip + 1, embed + taken(exchange(to_peers(trip), MP))

    _, embed = lax.while_loop(lambda state: state[0] < trips[0], another, (jnp.int32(1), taken(got)))

    normed = (standardize(embed) * in_gain).astype(bf16)
    everyone = to_everyone(normed, ACT)
    hidden = lax.dot_general(
        everyone.reshape(-1, width), up_rows, (((1,), (1,)), ((), ())), preferred_element_type=f32
    )
    active = jax.nn.gelu(hidden, approximate=False).astype(bf16)
    terms = jnp.dot(active, down_rows, preferred_element_type=f32).astype(bf16)
    terms = exchange(terms.reshape(everyone.shape), ACT)
    resid = normed.astype(f32) + jnp.sum(terms.astype(f32), axis=0)
    level = standardize(resid)
    score = jnp.sum(level * score_weight, axis=1)

    blocks = level.reshape(slots, peers, share).transpose(1, 0, 2).reshape(peers, 1, -1)
    score = jnp.broadcast_to(jnp.pad(score, (0, LANES - slots)), (peers, 1, LANES))
    got = exchange(jnp.concatenate([blocks, score], axis=2), MP)
    level = got[:, 0, : slots * share].reshape(peers, slots, share)
    by_spot = (level * out_gain).astype(bf16).transpose(1, 0, 2).reshape(toks, share)
    score = got[:, 0, slots * share :][:, :slots].T.reshape(1, toks)
    spot = spot.reshape(1, toks)
    where = spot == jnp.arange(toks)[:, None]
    encoded = lax.dot_general(
        by_spot, where.astype(bf16), (((0,), (0,)), ((), ())), preferred_element_type=f32
    )
    triple = jnp.arange(toks // seq_len)[:, None]
    of_triple = jnp.sum(jnp.where(where, jnp.arange(toks)[None] // seq_len, 0), axis=1)
    scores = jnp.sum(jnp.where(of_triple[None] == triple, score, 0.0), axis=1) / seq_len
    diff = jax.nn.sigmoid(scores) - labels.astype(f32)
    pooled = jnp.mean(encoded.reshape(share, toks // seq_len, seq_len), axis=2)
    grad = jnp.sum(diff[None] * pooled, axis=1)
    grad = grad + swapped(grad, "core")
    grad = grad + swapped(grad, "yl")
    return encoded.T.astype(bf16), scores, grad


def solution(mesh):
    parts = Mesh(mesh.devices.reshape(2, 2, 2, 4, 2, 4), (*DP, *MP))
    return jax.shard_map(
        on_device,
        mesh=parts,
        in_specs=(
            P(MP, None),
            P(DP, None),
            P(DP, None),
            P(DP),
            P(),
            P(None, MP),
            P(MP, None),
            P(MP),
            P(MP),
        ),
        out_specs=(P(DP, MP), P(DP), P(MP)),
        check_vma=False,
    )
```

```python
import functools

import jax
import jax.numpy as jnp
from jax import lax
from jax.experimental import pallas as pl
from jax.experimental.pallas import tpu as pltpu
from jax.sharding import Mesh
from jax.sharding import PartitionSpec as P

MP = ("yh", "zh", "zl", "x")
DP = ("yl", "core")
ACT = ("yh", "zl", "x")
LANES = 128
COVER = 40_000_000


def exchange(blocks, axes):
    return lax.all_to_all(blocks, axes, split_axis=0, concat_axis=0, tiled=True)


def to_everyone(array, axes):
    return exchange(jnp.broadcast_to(array, (lax.axis_size(axes), *array.shape)), axes)


def moved(array, axis, step):
    peers = lax.axis_size(axis)
    return lax.ppermute(array, axis, [((i + step) % peers, i) for i in range(peers)])


def swapped(array, axis):
    return lax.ppermute(array, axis, [(0, 1), (1, 0)])


def send_kernel(
    peers, place_ref, trip_ref, triples, words, gain, weight, table, sent, tiles, lanes, rows, held, sems
):
    lead, n_triples = triples.shape
    seq_len = lead + words.shape[1]
    entries, width = table.shape
    half = width // 2
    low = place_ref[0] * entries
    skipped = trip_ref[0] * peers
    group = 8

    def copy(number, local):
        start = pl.multiple_of((local >> 3) * 8, 8)
        return pltpu.make_async_copy(
            table.at[pl.ds(start, 8), :], tiles.at[number], sems.at[number]
        )

    held[0] = 0

    def scan(i, below):
        for g in range(0, seq_len, group):
            locals_ = [
                (triples[j, i] if j < lead else words[i, j - lead]) - low
                for j in range(g, g + group)
            ]
            outside = [local & -entries for local in locals_]
            any_mine = outside[0] == 0
            for out in outside[1:]:
                any_mine = any_mine | (out == 0)
            for local in locals_:
                below = below - (local >> 31)

            @pl.when(any_mine)
            def _(locals_=locals_, outside=outside):
                for local, out in zip(locals_, outside):
                    @pl.when(out == 0)
                    def _(local=local):
                        number = held[0] - skipped
                        held[0] = held[0] + 1

                        @pl.when((number >= 0) & (number < peers))
                        def _():
                            rows[number] = local
                            copy(number, local).start()

        return below

    below = lax.fori_loop(0, n_triples, scan, jnp.int32(0))

    lanes[...] = jnp.zeros_like(lanes)
    share = gain.shape[1]
    lanes[0:1, 0:share] = gain[...] * weight[...]
    exact = lanes[...]
    high = exact.astype(jnp.bfloat16).astype(jnp.float32)
    middle = (exact - high).astype(jnp.bfloat16).astype(jnp.float32)
    least = (exact - high - middle).astype(jnp.bfloat16).astype(jnp.float32)
    parts = high + pltpu.roll(middle, share, 1) + pltpu.roll(least, 2 * share, 1)
    row_of = lax.broadcasted_iota(jnp.int32, parts.shape, 0)
    slot_at = row_of == 1
    blank = jnp.where(slot_at, -1.0, parts)[0:2]
    sent[:, :, 0:half] = jnp.zeros((peers, 2, half), sent.dtype)
    sent[:, :, half:] = jnp.broadcast_to(blank[None], (peers, 2, LANES)).astype(sent.dtype)

    def place_row(number, carry):
        local = rows[number]
        copy(number, local).wait()
        tile = tiles[number].astype(jnp.float32)
        picked = lax.broadcasted_iota(jnp.int32, tile.shape, 0) == (local & 7)
        row = jnp.sum(jnp.where(picked, tile, 0.0), axis=0, keepdims=True)
        pair = jnp.concatenate([row[:, :half], row[:, half:]], axis=0)
        spot = below + skipped + number
        peer = spot & (peers - 1)
        slot = (spot // peers).astype(jnp.float32)
        sent[peer, :, 0:half] = pair.astype(sent.dtype)
        sent[peer, :, half:] = jnp.where(slot_at, slot, parts)[0:2].astype(sent.dtype)
        return carry

    here = jnp.clip(held[0] - skipped, 0, peers)
    lax.fori_loop(0, here, place_row, jnp.int32(0))


def to_send(place, trip, triples, words, gain, weight, table, peers):
    width = table.shape[1]
    vmem = pl.BlockSpec(memory_space=pltpu.VMEM)
    smem = pl.BlockSpec(memory_space=pltpu.SMEM)
    return pl.pallas_call(
        functools.partial(send_kernel, peers),
        out_shape=jax.ShapeDtypeStruct((peers, 2, width // 2 + LANES), table.dtype),
        in_specs=[smem] * 4 + [vmem] * 2 + [pl.BlockSpec(memory_space=pl.ANY)],
        out_specs=vmem,
        scratch_shapes=[
            pltpu.VMEM((peers, 8, width), table.dtype),
            pltpu.VMEM((8, LANES), jnp.float32),
            pltpu.SMEM((peers,), jnp.int32),
            pltpu.SMEM((1,), jnp.int32),
            pltpu.SemaphoreType.DMA((peers,)),
        ],
        name="send_rows",
    )(place.reshape(1), trip.reshape(1), triples.T, words, gain, weight, table)


def position_kernel(entries, peers, triples, words, words_v, after, spot_ref, trips_ref, ids_ref):
    n_triples, seq_len = spot_ref.shape
    lead = triples.shape[0]
    toks = n_triples * seq_len
    shift = entries.bit_length() - 1
    for j in range(lead):
        for i in range(n_triples):
            ids_ref[i : i + 1, j : j + 1] = jnp.full((1, 1), triples[j, i], jnp.int32)
    ids_ref[:, lead:] = words_v[...]
    least = (ids_ref[...] >> shift) * toks
    keys = least + lax.broadcasted_iota(jnp.int32, least.shape, 0) * seq_len
    keys = keys + lax.broadcasted_iota(jnp.int32, keys.shape, 1)

    def scan(i, carry):
        spot, first = carry
        for j in range(seq_len):
            token = triples[j, i] if j < lead else words[i, j - lead]
            key = (token >> shift) * toks + (i * seq_len + j)
            spot = spot + (key < keys).astype(jnp.int32)
            first = first + (key < least).astype(jnp.int32)
        return spot, first

    none = jnp.zeros(keys.shape, jnp.int32)
    spot, first = lax.fori_loop(0, n_triples, scan, (none, none))
    spot_ref[...] = spot
    trips_ref[0] = jnp.max((spot - first).astype(jnp.float32)).astype(jnp.int32) // peers + 1


def positions(triples, words, entries, peers, after):
    shape = (triples.shape[0], triples.shape[1] + words.shape[1])
    smem = pl.BlockSpec(memory_space=pltpu.SMEM)
    vmem = pl.BlockSpec(memory_space=pltpu.VMEM)
    return pl.pallas_call(
        functools.partial(position_kernel, entries, peers),
        out_shape=(
            jax.ShapeDtypeStruct(shape, jnp.int32),
            jax.ShapeDtypeStruct((1,), jnp.int32),
        ),
        in_specs=[smem, smem, vmem, pl.BlockSpec(memory_space=pl.ANY)],
        out_specs=(vmem, smem),
        cost_estimate=pl.CostEstimate(flops=0, transcendentals=0, bytes_accessed=COVER),
        scratch_shapes=[pltpu.VMEM(shape, jnp.int32)],
        name="positions",
    )(triples.T, words, words, after)


def standardize(values):
    width = values.shape[1]
    mean = jnp.sum(values, axis=1, keepdims=True) / width
    var = jnp.sum(values * values, axis=1, keepdims=True) / width - mean * mean
    return (values - mean) * lax.rsqrt(var + 1e-05)


def on_device(
    table, triples, words, labels, in_gain, up_weight, down_weight, out_gain, class_weight
):
    bf16, f32 = jnp.bfloat16, jnp.float32
    peers = lax.axis_size(MP)
    place = lax.axis_index(MP)
    seq_len = triples.shape[1] + words.shape[1]
    toks = triples.shape[0] * seq_len
    entries, width = table.shape
    slots = toks // peers
    share = width // peers

    units = up_weight.shape[1]
    half_units = units // lax.axis_size("core")
    start = lax.axis_index("core") * half_units
    own = lax.optimization_barrier(jnp.concatenate([up_weight.T, down_weight], axis=0))
    far = lax.dynamic_slice_in_dim(own.reshape(2, units, width), start, half_units, 1)
    far = moved(far.reshape(units, width), "zh", 2)
    weights = [own, moved(own, "zh", 1), moved(own, "zh", 3)]
    halves = [far, swapped(far, "core")]
    up_rows = jnp.concatenate(
        [w[:units] for w in weights] + [h[:half_units] for h in halves], axis=0
    )
    down_rows = jnp.concatenate(
        [w[units:] for w in weights] + [h[half_units:] for h in halves], axis=0
    )

    gains = out_gain.reshape(1, -1), class_weight.reshape(1, -1)

    def to_peers(trip):
        return to_send(place, trip, triples, words, *gains, table, peers)

    half = width // 2

    def taken(got):
        picks = got[:, 1, half : half + slots].astype(f32) == jnp.arange(slots, dtype=f32)[None]
        rows = jnp.concatenate([got[:, 0, :half], got[:, 1, :half]], axis=1)
        return lax.dot_general(
            picks.astype(bf16), rows, (((0,), (0,)), ((), ())), preferred_element_type=f32
        )

    sent = to_peers(jnp.int32(0))
    got = exchange(sent, MP)
    spot, trips = positions(triples, words, entries, peers, sent)
    score_weight = got[:, 0, half : half + 3 * share].astype(f32).reshape(peers, 3, share)
    score_weight = jnp.sum(score_weight, axis=1).reshape(1, width)

    def another(state):
        trip, embed = state
        return trip + 1, embed + taken(exchange(to_peers(trip), MP))

    _, embed = lax.while_loop(lambda state: state[0] < trips[0], another, (jnp.int32(1), taken(got)))

    normed = (standardize(embed) * in_gain).astype(bf16)
    everyone = to_everyone(normed, ACT)
    hidden = lax.dot_general(
        everyone.reshape(-1, width), up_rows, (((1,), (1,)), ((), ())), preferred_element_type=f32
    )
    active = jax.nn.gelu(hidden, approximate=False).astype(bf16)
    terms = jnp.dot(active, down_rows, preferred_element_type=f32).astype(bf16)
    terms = exchange(terms.reshape(everyone.shape), ACT)
    resid = normed.astype(f32) + jnp.sum(terms.astype(f32), axis=0)
    level = standardize(resid)
    score = jnp.sum(level * score_weight, axis=1)

    blocks = level.reshape(slots, peers, share).transpose(1, 0, 2).reshape(peers, 1, -1)
    score = jnp.broadcast_to(jnp.pad(score, (0, LANES - slots)), (peers, 1, LANES))
    got = exchange(jnp.concatenate([blocks, score], axis=2), MP)
    level = got[:, 0, : slots * share].reshape(peers, slots, share)
    by_spot = (level * out_gain).astype(bf16).transpose(1, 0, 2).reshape(toks, share)
    score = got[:, 0, slots * share :][:, :slots].T.reshape(1, toks)
    spot = spot.reshape(1, toks)
    where = spot == jnp.arange(toks)[:, None]
    encoded = lax.dot_general(
        by_spot, where.astype(bf16), (((0,), (0,)), ((), ())), preferred_element_type=f32
    )
    triple = jnp.arange(toks // seq_len)[:, None]
    of_triple = jnp.sum(jnp.where(where, jnp.arange(toks)[None] // seq_len, 0), axis=1)
    scores = jnp.sum(jnp.where(of_triple[None] == triple, score, 0.0), axis=1) / seq_len
    diff = jax.nn.sigmoid(scores) - labels.astype(f32)
    pooled = jnp.mean(encoded.reshape(share, toks // seq_len, seq_len), axis=2)
    grad = jnp.sum(diff[None] * pooled, axis=1)
    across = lax.ppermute(grad, DP, [(0, 3), (1, 2), (2, 1), (3, 0)])
    grad = (grad + swapped(grad, "core")) + (swapped(grad, "yl") + across)
    return encoded.T.astype(bf16), scores, grad


def solution(mesh):
    parts = Mesh(mesh.devices.reshape(2, 2, 2, 4, 2, 4), (*DP, *MP))
    return jax.shard_map(
        on_device,
        mesh=parts,
        in_specs=(
            P(MP, None),
            P(DP, None),
            P(DP, None),
            P(DP),
            P(),
            P(None, MP),
            P(MP, None),
            P(MP),
            P(MP),
        ),
        out_specs=(P(DP, MP), P(DP), P(MP)),
        check_vma=False,
    )
```

```python
import functools

import jax
import jax.numpy as jnp
from jax import lax
from jax.experimental import pallas as pl
from jax.experimental.pallas import tpu as pltpu
from jax.sharding import Mesh
from jax.sharding import PartitionSpec as P

MP = ("yh", "zh", "zl", "x")
DP = ("yl", "core")
ACT = ("yh", "zl", "x")
LANES = 128
COVER = 40_000_000


def exchange(blocks, axes):
    return lax.all_to_all(blocks, axes, split_axis=0, concat_axis=0, tiled=True)


def to_everyone(array, axes):
    return exchange(jnp.broadcast_to(array, (lax.axis_size(axes), *array.shape)), axes)


def moved(array, axis, step):
    peers = lax.axis_size(axis)
    return lax.ppermute(array, axis, [((i + step) % peers, i) for i in range(peers)])


def swapped(array, axis):
    return lax.ppermute(array, axis, [(0, 1), (1, 0)])


def send_kernel(
    peers, place_ref, trip_ref, triples, words, gain, weight, table, sent, tiles, lanes, rows, held, sems
):
    lead, n_triples = triples.shape
    seq_len = lead + words.shape[1]
    entries, width = table.shape
    half = width // 2
    low = place_ref[0] * entries
    skipped = trip_ref[0] * peers
    group = 8

    def copy(number, local):
        start = pl.multiple_of((local >> 3) * 8, 8)
        return pltpu.make_async_copy(
            table.at[pl.ds(start, 8), :], tiles.at[number], sems.at[number]
        )

    held[0] = 0

    def scan(i, below):
        for g in range(0, seq_len, group):
            locals_ = [
                (triples[j, i] if j < lead else words[i, j - lead]) - low
                for j in range(g, g + group)
            ]
            outside = [local & -entries for local in locals_]
            any_mine = outside[0] == 0
            for out in outside[1:]:
                any_mine = any_mine | (out == 0)
            for local in locals_:
                below = below - (local >> 31)

            @pl.when(any_mine)
            def _(locals_=locals_, outside=outside):
                for local, out in zip(locals_, outside):
                    @pl.when(out == 0)
                    def _(local=local):
                        number = held[0] - skipped
                        held[0] = held[0] + 1

                        @pl.when((number >= 0) & (number < peers))
                        def _():
                            rows[number] = local
                            copy(number, local).start()

        return below

    below = lax.fori_loop(0, n_triples, scan, jnp.int32(0))

    lanes[...] = jnp.zeros_like(lanes)
    share = gain.shape[1]
    lanes[0:1, 0:share] = gain[...] * weight[...]
    exact = lanes[...]
    high = exact.astype(jnp.bfloat16).astype(jnp.float32)
    middle = (exact - high).astype(jnp.bfloat16).astype(jnp.float32)
    least = (exact - high - middle).astype(jnp.bfloat16).astype(jnp.float32)
    parts = high + pltpu.roll(middle, share, 1) + pltpu.roll(least, 2 * share, 1)
    row_of = lax.broadcasted_iota(jnp.int32, parts.shape, 0)
    slot_at = row_of == 1
    blank = jnp.where(slot_at, -1.0, parts)[0:2]
    sent[:, :, 0:half] = jnp.zeros((peers, 2, half), sent.dtype)
    sent[:, :, half:] = jnp.broadcast_to(blank[None], (peers, 2, LANES)).astype(sent.dtype)

    def place_row(number, carry):
        local = rows[number]
        copy(number, local).wait()
        tile = tiles[number].astype(jnp.float32)
        picked = lax.broadcasted_iota(jnp.int32, tile.shape, 0) == (local & 7)
        row = jnp.sum(jnp.where(picked, tile, 0.0), axis=0, keepdims=True)
        pair = jnp.concatenate([row[:, :half], row[:, half:]], axis=0)
        spot = below + skipped + number
        peer = spot & (peers - 1)
        slot = (spot // peers).astype(jnp.float32)
        sent[peer, :, 0:half] = pair.astype(sent.dtype)
        sent[peer, :, half:] = jnp.where(slot_at, slot, parts)[0:2].astype(sent.dtype)
        return carry

    here = jnp.clip(held[0] - skipped, 0, peers)
    lax.fori_loop(0, here, place_row, jnp.int32(0))


def to_send(place, trip, triples, words, gain, weight, table, peers):
    width = table.shape[1]
    vmem = pl.BlockSpec(memory_space=pltpu.VMEM)
    smem = pl.BlockSpec(memory_space=pltpu.SMEM)
    return pl.pallas_call(
        functools.partial(send_kernel, peers),
        out_shape=jax.ShapeDtypeStruct((peers, 2, width // 2 + LANES), table.dtype),
        in_specs=[smem] * 4 + [vmem] * 2 + [pl.BlockSpec(memory_space=pl.ANY)],
        out_specs=vmem,
        scratch_shapes=[
            pltpu.VMEM((peers, 8, width), table.dtype),
            pltpu.VMEM((8, LANES), jnp.float32),
            pltpu.SMEM((peers,), jnp.int32),
            pltpu.SMEM((1,), jnp.int32),
            pltpu.SemaphoreType.DMA((peers,)),
        ],
        name="send_rows",
    )(place.reshape(1), trip.reshape(1), triples.T, words, gain, weight, table)


def position_kernel(entries, peers, triples, words, words_v, after, spot_ref, trips_ref, ids_ref):
    n_triples, seq_len = spot_ref.shape
    lead = triples.shape[0]
    toks = n_triples * seq_len
    shift = entries.bit_length() - 1
    for j in range(lead):
        for i in range(n_triples):
            ids_ref[i : i + 1, j : j + 1] = jnp.full((1, 1), triples[j, i], jnp.int32)
    ids_ref[:, lead:] = words_v[...]
    least = (ids_ref[...] >> shift) * toks
    keys = least + lax.broadcasted_iota(jnp.int32, least.shape, 0) * seq_len
    keys = keys + lax.broadcasted_iota(jnp.int32, keys.shape, 1)

    def scan(i, carry):
        spot, first = carry
        for j in range(seq_len):
            token = triples[j, i] if j < lead else words[i, j - lead]
            key = (token >> shift) * toks + (i * seq_len + j)
            spot = spot + (key < keys).astype(jnp.int32)
            first = first + (key < least).astype(jnp.int32)
        return spot, first

    none = jnp.zeros(keys.shape, jnp.int32)
    spot, first = lax.fori_loop(0, n_triples, scan, (none, none))
    spot_ref[...] = spot
    trips_ref[0] = jnp.max((spot - first).astype(jnp.float32)).astype(jnp.int32) // peers + 1


def positions(triples, words, entries, peers, after):
    shape = (triples.shape[0], triples.shape[1] + words.shape[1])
    smem = pl.BlockSpec(memory_space=pltpu.SMEM)
    vmem = pl.BlockSpec(memory_space=pltpu.VMEM)
    return pl.pallas_call(
        functools.partial(position_kernel, entries, peers),
        out_shape=(
            jax.ShapeDtypeStruct(shape, jnp.int32),
            jax.ShapeDtypeStruct((1,), jnp.int32),
        ),
        in_specs=[smem, smem, vmem, pl.BlockSpec(memory_space=pl.ANY)],
        out_specs=(vmem, smem),
        cost_estimate=pl.CostEstimate(flops=0, transcendentals=0, bytes_accessed=COVER),
        scratch_shapes=[pltpu.VMEM(shape, jnp.int32)],
        name="positions",
    )(triples.T, words, words, after)


def standardize(values):
    width = values.shape[1]
    mean = jnp.sum(values, axis=1, keepdims=True) / width
    var = jnp.sum(values * values, axis=1, keepdims=True) / width - mean * mean
    return (values - mean) * lax.rsqrt(var + 1e-05)


def on_device(
    table, triples, words, labels, in_gain, up_weight, down_weight, out_gain, class_weight
):
    bf16, f32 = jnp.bfloat16, jnp.float32
    peers = lax.axis_size(MP)
    place = lax.axis_index(MP)
    seq_len = triples.shape[1] + words.shape[1]
    toks = triples.shape[0] * seq_len
    entries, width = table.shape
    slots = toks // peers
    share = width // peers

    units = up_weight.shape[1]
    half_units = units // lax.axis_size("core")
    start = lax.axis_index("core") * half_units
    own = lax.optimization_barrier(jnp.concatenate([up_weight.T, down_weight], axis=0))
    far = lax.dynamic_slice_in_dim(own.reshape(2, units, width), start, half_units, 1)
    far = moved(far.reshape(units, width), "zh", 2)
    weights = [own, moved(own, "zh", 1), moved(own, "zh", 3)]
    halves = [far, swapped(far, "core")]
    up_rows = jnp.concatenate(
        [w[:units] for w in weights] + [h[:half_units] for h in halves], axis=0
    )
    down_rows = jnp.concatenate(
        [w[units:] for w in weights] + [h[half_units:] for h in halves], axis=0
    )

    gains = out_gain.reshape(1, -1), class_weight.reshape(1, -1)

    def to_peers(trip):
        return to_send(place, trip, triples, words, *gains, table, peers)

    half = width // 2

    def taken(got):
        picks = got[:, 1, half : half + slots].astype(f32) == jnp.arange(slots, dtype=f32)[None]
        rows = jnp.concatenate([got[:, 0, :half], got[:, 1, :half]], axis=1)
        return lax.dot_general(
            picks.astype(bf16), rows, (((0,), (0,)), ((), ())), preferred_element_type=f32
        )

    sent = to_peers(jnp.int32(0))
    got = exchange(sent, MP)
    spot, trips = positions(triples, words, entries, peers, sent)
    score_weight = got[:, 0, half : half + 3 * share].astype(f32).reshape(peers, 3, share)
    score_weight = jnp.sum(score_weight, axis=1).reshape(1, width)

    def another(state):
        trip, embed = state
        return trip + 1, embed + taken(exchange(to_peers(trip), MP))

    _, embed = lax.while_loop(lambda state: state[0] < trips[0], another, (jnp.int32(1), taken(got)))

    normed = (standardize(embed) * in_gain).astype(bf16)
    everyone = to_everyone(normed, ACT)
    hidden = lax.dot_general(
        everyone.reshape(-1, width), up_rows, (((1,), (1,)), ((), ())), preferred_element_type=f32
    )
    active = jax.nn.gelu(hidden, approximate=False).astype(bf16)
    terms = jnp.dot(active, down_rows, preferred_element_type=f32).astype(bf16)
    terms = exchange(terms.reshape(everyone.shape), ACT)
    resid = normed.astype(f32) + jnp.sum(terms.astype(f32), axis=0)
    level = standardize(resid)
    score = jnp.sum(level * score_weight, axis=1)

    blocks = level.reshape(slots, peers, share).transpose(1, 0, 2).reshape(peers, 1, -1)
    score = jnp.broadcast_to(jnp.pad(score, (0, LANES - slots)), (peers, 1, LANES))
    got = exchange(jnp.concatenate([blocks, score], axis=1), MP)
    level = got[:, 0].reshape(peers, slots, share)
    by_spot = (level * out_gain).astype(bf16).transpose(1, 0, 2).reshape(toks, share)
    score = got[:, 1, :slots].T.reshape(1, toks)
    spot = spot.reshape(1, toks)
    where = spot == jnp.arange(toks)[:, None]
    encoded = lax.dot_general(
        by_spot, where.astype(bf16), (((0,), (0,)), ((), ())), preferred_element_type=f32
    )
    triple = jnp.arange(toks // seq_len)[:, None]
    of_triple = jnp.sum(jnp.where(where, jnp.arange(toks)[None] // seq_len, 0), axis=1)
    scores = jnp.sum(jnp.where(of_triple[None] == triple, score, 0.0), axis=1) / seq_len
    diff = jax.nn.sigmoid(scores) - labels.astype(f32)
    pooled = jnp.mean(encoded.reshape(share, toks // seq_len, seq_len), axis=2)
    grad = jnp.sum(diff[None] * pooled, axis=1)
    across = lax.ppermute(grad, DP, [(0, 3), (1, 2), (2, 1), (3, 0)])
    grad = (grad + swapped(grad, "core")) + (swapped(grad, "yl") + across)
    return encoded.T.astype(bf16), scores, grad


def solution(mesh):
    parts = Mesh(mesh.devices.reshape(2, 2, 2, 4, 2, 4), (*DP, *MP))
    return jax.shard_map(
        on_device,
        mesh=parts,
        in_specs=(
            P(MP, None),
            P(DP, None),
            P(DP, None),
            P(DP),
            P(),
            P(None, MP),
            P(MP, None),
            P(MP),
            P(MP),
        ),
        out_specs=(P(DP, MP), P(DP), P(MP)),
        check_vma=False,
    )
```

```python
import functools

import jax
import jax.numpy as jnp
from jax import lax
from jax.experimental import pallas as pl
from jax.experimental.pallas import tpu as pltpu
from jax.sharding import Mesh
from jax.sharding import PartitionSpec as P

MP = ("yh", "zh", "zl", "x")
DP = ("yl", "core")
ACT = ("yh", "zl", "x")
LANES = 128
COVER = 40_000_000


def exchange(blocks, axes):
    return lax.all_to_all(blocks, axes, split_axis=0, concat_axis=0, tiled=True)


def to_everyone(array, axes):
    return exchange(jnp.broadcast_to(array, (lax.axis_size(axes), *array.shape)), axes)


def moved(array, axis, step):
    peers = lax.axis_size(axis)
    return lax.ppermute(array, axis, [((i + step) % peers, i) for i in range(peers)])


def swapped(array, axis):
    return lax.ppermute(array, axis, [(0, 1), (1, 0)])


def send_kernel(
    peers, place_ref, trip_ref, triples, words, gain, weight, table, sent, tiles, lanes, rows, held, sems
):
    lead, n_triples = triples.shape
    seq_len = lead + words.shape[1]
    entries, width = table.shape
    half = width // 2
    low = place_ref[0] * entries
    skipped = trip_ref[0] * peers
    group = 8

    def copy(number, local):
        start = pl.multiple_of((local >> 3) * 8, 8)
        return pltpu.make_async_copy(
            table.at[pl.ds(start, 8), :], tiles.at[number], sems.at[number]
        )

    held[0] = 0

    def scan(i, below):
        for g in range(0, seq_len, group):
            locals_ = [
                (triples[j, i] if j < lead else words[i, j - lead]) - low
                for j in range(g, g + group)
            ]
            outside = [local & -entries for local in locals_]
            any_mine = outside[0] == 0
            for out in outside[1:]:
                any_mine = any_mine | (out == 0)
            for local in locals_:
                below = below - (local >> 31)

            @pl.when(any_mine)
            def _(locals_=locals_, outside=outside):
                for local, out in zip(locals_, outside):
                    @pl.when(out == 0)
                    def _(local=local):
                        number = held[0] - skipped
                        held[0] = held[0] + 1

                        @pl.when((number >= 0) & (number < peers))
                        def _():
                            rows[number] = local
                            copy(number, local).start()

        return below

    below = lax.fori_loop(0, n_triples, scan, jnp.int32(0))

    lanes[...] = jnp.zeros_like(lanes)
    share = gain.shape[1]
    lanes[0:1, 0:share] = gain[...] * weight[...]
    exact = lanes[...]
    high = exact.astype(jnp.bfloat16).astype(jnp.float32)
    middle = (exact - high).astype(jnp.bfloat16).astype(jnp.float32)
    least = (exact - high - middle).astype(jnp.bfloat16).astype(jnp.float32)
    parts = high + pltpu.roll(middle, share, 1) + pltpu.roll(least, 2 * share, 1)
    row_of = lax.broadcasted_iota(jnp.int32, parts.shape, 0)
    slot_at = row_of == 1
    blank = jnp.where(slot_at, -1.0, parts)[0:2]
    sent[:, :, 0:half] = jnp.zeros((peers, 2, half), sent.dtype)
    sent[:, :, half:] = jnp.broadcast_to(blank[None], (peers, 2, LANES)).astype(sent.dtype)

    def place_row(number, carry):
        local = rows[number]
        copy(number, local).wait()
        tile = tiles[number].astype(jnp.float32)
        picked = lax.broadcasted_iota(jnp.int32, tile.shape, 0) == (local & 7)
        row = jnp.sum(jnp.where(picked, tile, 0.0), axis=0, keepdims=True)
        pair = jnp.concatenate([row[:, :half], row[:, half:]], axis=0)
        spot = below + skipped + number
        peer = spot & (peers - 1)
        slot = (spot // peers).astype(jnp.float32)
        sent[peer, :, 0:half] = pair.astype(sent.dtype)
        sent[peer, :, half:] = jnp.where(slot_at, slot, parts)[0:2].astype(sent.dtype)
        return carry

    here = jnp.clip(held[0] - skipped, 0, peers)
    lax.fori_loop(0, here, place_row, jnp.int32(0))


def to_send(place, trip, triples, words, gain, weight, table, peers):
    width = table.shape[1]
    vmem = pl.BlockSpec(memory_space=pltpu.VMEM)
    smem = pl.BlockSpec(memory_space=pltpu.SMEM)
    return pl.pallas_call(
        functools.partial(send_kernel, peers),
        out_shape=jax.ShapeDtypeStruct((peers, 2, width // 2 + LANES), table.dtype),
        in_specs=[smem] * 4 + [vmem] * 2 + [pl.BlockSpec(memory_space=pl.ANY)],
        out_specs=vmem,
        scratch_shapes=[
            pltpu.VMEM((peers, 8, width), table.dtype),
            pltpu.VMEM((8, LANES), jnp.float32),
            pltpu.SMEM((peers,), jnp.int32),
            pltpu.SMEM((1,), jnp.int32),
            pltpu.SemaphoreType.DMA((peers,)),
        ],
        name="send_rows",
    )(place.reshape(1), trip.reshape(1), triples.T, words, gain, weight, table)


def position_kernel(entries, peers, triples, words, words_v, after, spot_ref, trips_ref, ids_ref):
    n_triples, seq_len = spot_ref.shape
    lead = triples.shape[0]
    toks = n_triples * seq_len
    shift = entries.bit_length() - 1
    for j in range(lead):
        for i in range(n_triples):
            ids_ref[i : i + 1, j : j + 1] = jnp.full((1, 1), triples[j, i], jnp.int32)
    ids_ref[:, lead:] = words_v[...]
    least = (ids_ref[...] >> shift) * toks
    keys = least + lax.broadcasted_iota(jnp.int32, least.shape, 0) * seq_len
    keys = keys + lax.broadcasted_iota(jnp.int32, keys.shape, 1)

    def scan(i, carry):
        spot, first = carry
        for j in range(seq_len):
            token = triples[j, i] if j < lead else words[i, j - lead]
            key = (token >> shift) * toks + (i * seq_len + j)
            spot = spot + (key < keys).astype(jnp.int32)
            first = first + (key < least).astype(jnp.int32)
        return spot, first

    none = jnp.zeros(keys.shape, jnp.int32)
    spot, first = lax.fori_loop(0, n_triples, scan, (none, none))
    spot_ref[...] = spot
    trips_ref[0] = jnp.max((spot - first).astype(jnp.float32)).astype(jnp.int32) // peers + 1


def positions(triples, words, entries, peers, after):
    shape = (triples.shape[0], triples.shape[1] + words.shape[1])
    smem = pl.BlockSpec(memory_space=pltpu.SMEM)
    vmem = pl.BlockSpec(memory_space=pltpu.VMEM)
    return pl.pallas_call(
        functools.partial(position_kernel, entries, peers),
        out_shape=(
            jax.ShapeDtypeStruct(shape, jnp.int32),
            jax.ShapeDtypeStruct((1,), jnp.int32),
        ),
        in_specs=[smem, smem, vmem, pl.BlockSpec(memory_space=pl.ANY)],
        out_specs=(vmem, smem),
        cost_estimate=pl.CostEstimate(flops=0, transcendentals=0, bytes_accessed=COVER),
        scratch_shapes=[pltpu.VMEM(shape, jnp.int32)],
        name="positions",
    )(triples.T, words, words, after)


def standardize(values):
    width = values.shape[1]
    mean = jnp.sum(values, axis=1, keepdims=True) / width
    var = jnp.sum(values * values, axis=1, keepdims=True) / width - mean * mean
    return (values - mean) * lax.rsqrt(var + 1e-05)


def on_device(
    table, triples, words, labels, in_gain, up_weight, down_weight, out_gain, class_weight
):
    bf16, f32 = jnp.bfloat16, jnp.float32
    peers = lax.axis_size(MP)
    place = lax.axis_index(MP)
    seq_len = triples.shape[1] + words.shape[1]
    toks = triples.shape[0] * seq_len
    entries, width = table.shape
    slots = toks // peers
    share = width // peers

    units = up_weight.shape[1]
    half_units = units // lax.axis_size("core")
    start = lax.axis_index("core") * half_units
    own = lax.optimization_barrier(jnp.concatenate([up_weight.T, down_weight], axis=0))
    far = lax.dynamic_slice_in_dim(own.reshape(2, units, width), start, half_units, 1)
    far = moved(far.reshape(units, width), "zh", 2)
    weights = [own, moved(own, "zh", 1), moved(own, "zh", 3)]
    halves = [far, swapped(far, "core")]
    up_rows = jnp.concatenate(
        [w[:units] for w in weights] + [h[:half_units] for h in halves], axis=0
    )
    down_rows = jnp.concatenate(
        [w[units:] for w in weights] + [h[half_units:] for h in halves], axis=0
    )

    gains = out_gain.reshape(1, -1), class_weight.reshape(1, -1)

    def to_peers(trip):
        return to_send(place, trip, triples, words, *gains, table, peers)

    half = width // 2

    def taken(got):
        picks = got[:, 1, half : half + slots].astype(f32) == jnp.arange(slots, dtype=f32)[None]
        rows = jnp.concatenate([got[:, 0, :half], got[:, 1, :half]], axis=1)
        return lax.dot_general(
            picks.astype(bf16), rows, (((0,), (0,)), ((), ())), preferred_element_type=f32
        )

    sent = to_peers(jnp.int32(0))
    got = exchange(sent, MP)
    spot, trips = positions(triples, words, entries, peers, sent)
    score_weight = got[:, 0, half : half + 3 * share].astype(f32).reshape(peers, 3, share)
    score_weight = jnp.sum(score_weight, axis=1).reshape(1, width)

    def another(state):
        trip, embed = state
        return trip + 1, embed + taken(exchange(to_peers(trip), MP))

    _, embed = lax.while_loop(lambda state: state[0] < trips[0], another, (jnp.int32(1), taken(got)))

    normed = (standardize(embed) * in_gain).astype(bf16)
    everyone = to_everyone(normed, ACT)
    hidden = lax.dot_general(
        everyone.reshape(-1, width), up_rows, (((1,), (1,)), ((), ())), preferred_element_type=f32
    )
    active = jax.nn.gelu(hidden, approximate=False).astype(bf16)
    terms = jnp.dot(active, down_rows, preferred_element_type=f32).astype(bf16)
    terms = exchange(terms.reshape(everyone.shape), ACT)
    resid = normed.astype(f32) + jnp.sum(terms.astype(f32), axis=0)
    level = standardize(resid)
    score = jnp.sum(level * score_weight, axis=1)

    blocks = level.reshape(slots, peers, share).transpose(1, 0, 2).reshape(peers, 1, -1)
    score = jnp.broadcast_to(jnp.pad(score, (0, LANES - slots)), (peers, 1, LANES))
    got = exchange(jnp.concatenate([blocks, score], axis=1), MP)
    level = got[:, 0].reshape(peers, slots, share)
    by_spot = (level * out_gain).astype(bf16).transpose(1, 0, 2).reshape(toks, share)
    score = got[:, 1, :slots].T.reshape(1, toks)
    spot = spot.reshape(1, toks)
    where = spot == jnp.arange(toks)[:, None]
    encoded = lax.dot_general(
        by_spot, where.astype(bf16), (((0,), (0,)), ((), ())), preferred_element_type=bf16
    )
    triple = jnp.arange(toks // seq_len)[:, None]
    of_triple = jnp.sum(jnp.where(where, jnp.arange(toks)[None] // seq_len, 0), axis=1)
    scores = jnp.sum(jnp.where(of_triple[None] == triple, score, 0.0), axis=1) / seq_len
    diff = jax.nn.sigmoid(scores) - labels.astype(f32)
    pooled = jnp.mean(encoded.astype(f32).reshape(share, toks // seq_len, seq_len), axis=2)
    grad = jnp.sum(diff[None] * pooled, axis=1)
    across = lax.ppermute(grad, DP, [(0, 3), (1, 2), (2, 1), (3, 0)])
    grad = (grad + swapped(grad, "core")) + (swapped(grad, "yl") + across)
    return encoded.T, scores, grad


def solution(mesh):
    parts = Mesh(mesh.devices.reshape(2, 2, 2, 4, 2, 4), (*DP, *MP))
    return jax.shard_map(
        on_device,
        mesh=parts,
        in_specs=(
            P(MP, None),
            P(DP, None),
            P(DP, None),
            P(DP),
            P(),
            P(None, MP),
            P(MP, None),
            P(MP),
            P(MP),
        ),
        out_specs=(P(DP, MP), P(DP), P(MP)),
        check_vma=False,
    )
```
